256 devices in a mesh: gx: 32 (over z, y), gy: 8 (over x, core).
Axes of the slice: x: 4, y: 4, z: 8, core: 2. Of those that a mesh axis runs over, the one named last changes fastest.
Arguments:
- samples_a: bfloat16 [32, 8, 64, 2048], P('gx', 'gy'), may hold values from -6 to 6
- samples_b: bfloat16 [32, 8, 64, 2048], P('gx', 'gy'), may hold values from -6 to 6
- count_a: int32 [32, 8, 512], P('gx', 'gy'), may hold values from 1 to 4
- count_b: int32 [32, 8, 512], P('gx', 'gy'), may hold values from 1 to 4
- sign_a: int32 [8, 512], P('gy'), may hold values from 0 to 1
- sign_b: int32 [32, 512], P('gx'), may hold values from 0 to 1
- slot_a: int32 [8, 512], P('gy'), may hold values from 0 to 511, each once within a row
- slot_b: int32 [32, 512], P('gx'), may hold values from 0 to 511, each once within a row
- target_a: float32 [8, 64, 512], P('gy'), may hold values from -4 to 4
- target_b: float32 [32, 64, 512], P('gx'), may hold values from -4 to 4
- w_in: bfloat16 [32, 8, 64, 256], P('gx', 'gy'), may hold values from -0.75 to 0.75
- b_in: float32 [32, 8, 256], P('gx', 'gy'), may hold values from -3 to 3
- w_mid: bfloat16 [32, 8, 256, 256], P('gx', 'gy'), may hold values from -0.375 to 0.375
- b_mid: float32 [32, 8, 256], P('gx', 'gy'), may hold values from -3 to 3
- w_feat: bfloat16 [32, 8, 256, 64], P('gx', 'gy'), may hold values from -0.375 to 0.375
- w_density: bfloat16 [32, 8, 256], P('gx', 'gy'), may hold values from -0.75 to 0.75
Outputs:
- pixel_a: float32 [8, 64, 512], P('gy', None, 'gx')
- pixel_b: float32 [32, 64, 512], P('gx', None, 'gy')
- grad_w_in: float32 [32, 8, 64, 256], P('gx', 'gy')
- grad_b_in: float32 [32, 8, 256], P('gx', 'gy')
- grad_w_mid: float32 [32, 8, 256, 256], P('gx', 'gy')
- grad_b_mid: float32 [32, 8, 256], P('gx', 'gy')
- grad_w_feat: float32 [32, 8, 256, 64], P('gx', 'gy')
- grad_w_density: float32 [32, 8, 256], P('gx', 'gy')
The draws below stay inside these ranges and needn't reach their ends.
Inputs may be any that keep to these rules, and one draw needn't show every extreme that they name: `count_a`: number of a ray's sample slots that lie in the block; they are the slots s < count. `count_b`: number of a ray's sample slots that lie in the block; they are the slots s < count. `sign_a`: 1: the ray crosses its line's blocks in increasing index along gx and its slots in increasing s; 0: both decreasing. `sign_b`: 1: the ray crosses its line's blocks in increasing index along gy and its slots in increasing s; 0: both decreasing. `slot_a`: each line's row is a permutation of the pixels. `slot_b`: each line's row is a permutation of the pixels.
All inputs are finite; a program needn't handle non-finite values.
Results may differ from the reference program's by a relative error of at most 0.01.
The reference program's roundings to bfloat16 on the way (of `hidden_one`, `hidden_two`, `d_feature`, `d_density`, `d_pre_two` and `d_pre_one`) count: a program that leaves them out, or rounds other values in their place, can miss the bound.
Values sent between devices are 32-bit elements; how exact they have to be, the bound alone decides.
A program may use at most 64 MiB of HBM per device.

```python
import jax
import jax.numpy as jnp
from jax import lax

IN = 64
H = 256
CH = 64
S = 4
R = 512
BX = 32
BY = 8


def set_ends(entries, key, low, largest):
    spot = [jax.random.randint(jax.random.fold_in(key, axis), (), 0, length) for axis, length in enumerate(entries.shape)]
    longest = entries.shape.index(max(entries.shape))
    neighbour = spot[:longest] + [(spot[longest] + 1) % entries.shape[longest]] + spot[longest + 1:]
    return entries.at[tuple(spot)].set(low).at[tuple(neighbour)].set(largest)


def shard_levels(key, shape, shards, low, high):
    gain, own = 1.0, jax.random.fold_in(key, 6)
    for axis_at, shards_of in shards:
        draws = jnp.exp(jax.random.uniform(jax.random.fold_in(own, axis_at), (shards_of,), jnp.float32, low / len(shards), high / len(shards)))
        gain = gain * jnp.repeat(draws, shape[axis_at] // shards_of).reshape([-1 if axis == axis_at else 1 for axis in range(len(shape))])
    return gain


def bell_draw(rng, dims, scale, most, split=(), held_as=jnp.bfloat16):
    loudness = shard_levels(rng, dims, split, -0.22, 0.18) if split else 1.0
    result = jax.random.normal(rng, dims, jnp.float32) * scale * loudness
    return jnp.minimum(jnp.maximum(result, -most), most).astype(held_as)


def setup_inputs(seed: int = 0) -> dict:
    keys = jax.random.split(jax.random.key(seed), 17)
    samples_a = bell_draw(keys[0], (BX, BY, IN, S * R), 1.0, 6.0, ((0, 32), (1, 8)))
    samples_b = bell_draw(keys[1], (BX, BY, IN, S * R), 1.0, 6.0, ((0, 32), (1, 8)))
    count_a = set_ends(jax.random.randint(keys[2], (BX, BY, R), 1, S + 1), jax.random.fold_in(keys[2], 1), 1, S).astype(jnp.int32)
    count_b = set_ends(jax.random.randint(keys[3], (BX, BY, R), 1, S + 1), jax.random.fold_in(keys[3], 1), 1, S).astype(jnp.int32)
    sign_a = set_ends(jax.random.randint(keys[4], (BY, R), 0, 2), jax.random.fold_in(keys[4], 1), 0, 1).astype(jnp.int32)
    sign_b = set_ends(jax.random.randint(keys[5], (BX, R), 0, 2), jax.random.fold_in(keys[5], 1), 0, 1).astype(jnp.int32)
    slot_a = jax.vmap(lambda own: jax.random.permutation(own, R))(jax.random.split(keys[6], BY)).reshape((BY, R)).astype(jnp.int32)
    slot_b = jax.vmap(lambda own: jax.random.permutation(own, R))(jax.random.split(keys[7], BX)).reshape((BX, R)).astype(jnp.int32)
    target_a = bell_draw(keys[8], (BY, CH, R), 0.5, 4.0, ((0, 8),), jnp.float32)
    target_b = bell_draw(keys[9], (BX, CH, R), 0.5, 4.0, ((0, 32),), jnp.float32)
    w_in = bell_draw(keys[10], (BX, BY, IN, H), IN ** -0.5, 0.75, ((0, 32), (1, 8)))
    b_in = bell_draw(keys[11], (BX, BY, H), 0.5, 3.0, ((0, 32), (1, 8)), jnp.float32)
    w_mid = bell_draw(keys[12], (BX, BY, H, H), H ** -0.5, 0.375, ((0, 32), (1, 8)))
    b_mid = bell_draw(keys[13], (BX, BY, H), 0.5, 3.0, ((0, 32), (1, 8)), jnp.float32)
    w_feat = bell_draw(keys[14], (BX, BY, H, CH), H ** -0.5, 0.375, ((0, 32), (1, 8)))
    w_density = bell_draw(keys[15], (BX, BY, H), (2.0 / H ** 0.5), 0.75, ((0, 32), (1, 8)))
    return {"samples_a": samples_a, "samples_b": samples_b, "count_a": count_a, "count_b": count_b, "sign_a": sign_a, "sign_b": sign_b, "slot_a": slot_a, "slot_b": slot_b, "target_a": target_a, "target_b": target_b, "w_in": w_in, "b_in": b_in, "w_mid": w_mid, "b_mid": b_mid, "w_feat": w_feat, "w_density": w_density}


optical_depth = 3.0
highest = lax.Precision.HIGHEST


def forward_mlp(encoded, weights):
    w_in, b_in, w_mid, b_mid, w_feat, w_density = weights
    pre_one = jnp.einsum("ih,in->hn", w_in.astype(jnp.float32), encoded.astype(jnp.float32), precision=highest) + b_in[:, None]
    hidden_one = jnp.maximum(pre_one, 0.0).astype(jnp.bfloat16)
    pre_two = jnp.einsum("gh,gn->hn", w_mid.astype(jnp.float32), hidden_one.astype(jnp.float32), precision=highest) + b_mid[:, None]
    hidden_two = jnp.maximum(pre_two, 0.0).astype(jnp.bfloat16)
    feature = jnp.einsum("hc,hn->cn", w_feat.astype(jnp.float32), hidden_two.astype(jnp.float32), precision=highest)
    density = jnp.einsum("h,hn->n", w_density.astype(jnp.float32), hidden_two.astype(jnp.float32), precision=highest)
    return hidden_one, hidden_two, feature, density


def segment(feature, density, counts, plus_ray, delta):
    ray_total = counts.shape[0]
    per_ray = density.shape[0] // ray_total
    masked = (jnp.arange(per_ray, dtype=jnp.int32)[:, None] < counts[None, :]).astype(jnp.float32)
    optical = delta * jax.nn.softplus(density.reshape(per_ray, ray_total)) * masked
    running = jnp.cumsum(optical, 0)
    before = jnp.where(plus_ray[None], running - optical, running[-1][None] - running)
    weight = jnp.exp(-before) * (-jnp.expm1(-optical))
    colour = feature.reshape(feature.shape[0], per_ray, ray_total)
    colour_seg = jnp.einsum("sr,csr->cr", weight, colour, precision=highest)
    return -running[-1], colour_seg, (masked, before, optical, weight, colour, density)


def segment_back(saved, d_colour, d_log, plus_ray, delta):
    masked, before, optical, weight, colour, density = saved
    channels = d_colour.shape[0]
    d_feature = (weight[None] * d_colour[:, None, :]).reshape(channels, -1).astype(jnp.bfloat16)
    d_weight = jnp.einsum("csr,cr->sr", colour, d_colour, precision=highest)
    product = d_weight * weight
    running = jnp.cumsum(product, 0)
    later_sum = jnp.where(plus_ray[None], running[-1][None] - running, running - product)
    d_optical = -d_log[None] + jnp.exp(-(before + optical)) * d_weight - later_sum
    slopes = jax.nn.sigmoid(density.reshape(masked.shape))
    d_density = (d_optical * delta * masked * slopes).reshape(-1).astype(jnp.bfloat16)
    return d_feature, d_density


def backward_mlp(encoded, hidden_one, hidden_two, weights, d_feature, d_density):
    w_in, b_in, w_mid, b_mid, w_feat, w_density = weights
    hidden_two_f = hidden_two.astype(jnp.float32)
    hidden_one_f = hidden_one.astype(jnp.float32)
    d_feature_f = d_feature.astype(jnp.float32)
    d_density_f = d_density.astype(jnp.float32)
    grad_feat = jnp.einsum("hn,cn->hc", hidden_two_f, d_feature_f, precision=highest)
    grad_dens = jnp.einsum("hn,n->h", hidden_two_f, d_density_f, precision=highest)
    d_two = jnp.einsum("hc,cn->hn", w_feat.astype(jnp.float32), d_feature_f, precision=highest)
    d_two = d_two + w_density.astype(jnp.float32)[:, None] * d_density_f[None, :]
    d_pre_two = jnp.where(hidden_two_f > 0, d_two, 0.0).astype(jnp.bfloat16)
    d_pre_two_f = d_pre_two.astype(jnp.float32)
    grad_mid = jnp.einsum("gn,hn->gh", hidden_one_f, d_pre_two_f, precision=highest)
    grad_bmid = jnp.sum(d_pre_two_f, 1)
    d_one = jnp.einsum("gh,hn->gn", w_mid.astype(jnp.float32), d_pre_two_f, precision=highest)
    d_pre_one = jnp.where(hidden_one_f > 0, d_one, 0.0).astype(jnp.bfloat16)
    d_pre_one_f = d_pre_one.astype(jnp.float32)
    grad_in = jnp.einsum("in,hn->ih", encoded.astype(jnp.float32), d_pre_one_f, precision=highest)
    grad_bin = jnp.sum(d_pre_one_f, 1)
    return grad_in, grad_bin, grad_mid, grad_bmid, grad_feat, grad_dens


def chain(log_seg, colour_seg, plus_ray, target, slots):
    flip_log = jnp.where(plus_ray[None], log_seg, log_seg[::-1])
    flip_colour = jnp.where(plus_ray[None, :, None, :], colour_seg, colour_seg[::-1])
    running = jnp.cumsum(flip_log, 0)
    front = jnp.exp(running - flip_log)
    pixels = jnp.sum(front[:, :, None, :] * flip_colour, 0)
    transmit = jnp.exp(flip_log)

    def advance(carried, block_item):
        trans_one, colour_one = block_item
        return colour_one + trans_one[:, None, :] * carried, carried

    _, behind = lax.scan(advance, jnp.zeros_like(flip_colour[0]), (transmit, flip_colour), reverse=True)
    picked = jnp.broadcast_to(slots[:, None, :], target.shape)
    residual = pixels - jnp.take_along_axis(target, picked, axis=2)
    d_colour = front[:, :, None, :] * residual[None]
    d_log = front * transmit * jnp.sum(residual[None] * behind, 2)
    d_colour = jnp.where(plus_ray[None, :, None, :], d_colour, d_colour[::-1])
    d_log = jnp.where(plus_ray[None], d_log, d_log[::-1])
    inverse = jnp.argsort(slots, axis=1).astype(jnp.int32)
    positions = jnp.broadcast_to(inverse[:, None, :], target.shape)
    return jnp.take_along_axis(pixels, positions, axis=2), d_colour, d_log


def reference(samples_a, samples_b, count_a, count_b, sign_a, sign_b, slot_a, slot_b, target_a, target_b, w_in, b_in, w_mid, b_mid, w_feat, w_density):
    blocks = BX * BY
    plus_a = jnp.broadcast_to((sign_a == 1)[None], (BX, BY, R))
    plus_b = jnp.broadcast_to((sign_b == 1)[:, None], (BX, BY, R))
    delta_a = optical_depth / (BX * S)
    delta_b = optical_depth / (BY * S)

    def flatten(tensor):
        return tensor.reshape((blocks,) + tensor.shape[2:])

    inputs = tuple(flatten(tensor) for tensor in (samples_a, samples_b, count_a, count_b, plus_a, plus_b, w_in, b_in, w_mid, b_mid, w_feat, w_density))

    def forward_block(block_item):
        joined = jnp.concatenate([block_item[0], block_item[1]], 1)
        hidden_one, hidden_two, feature, density = forward_mlp(joined, block_item[6:12])
        split_at = block_item[0].shape[1]
        seg_a = segment(feature[:, :split_at], density[:split_at], block_item[2], block_item[4], delta_a)
        seg_b = segment(feature[:, split_at:], density[split_at:], block_item[3], block_item[5], delta_b)
        return joined, hidden_one, hidden_two, seg_a, seg_b

    def first_pass(block_item):
        outcome = forward_block(block_item)
        return outcome[3][0], outcome[3][1], outcome[4][0], outcome[4][1]

    log_a, colour_a, log_b, colour_b = lax.map(first_pass, inputs)
    log_a = log_a.reshape(BX, BY, R)
    colour_a = colour_a.reshape(BX, BY, CH, R)
    log_b = log_b.reshape(BX, BY, R)
    colour_b = colour_b.reshape(BX, BY, CH, R)
    pixel_a, d_colour_a, d_log_a = chain(log_a, colour_a, sign_a == 1, target_a, slot_a)
    pixel_b, d_colour_b, d_log_b = chain(jnp.swapaxes(log_b, 0, 1), jnp.swapaxes(colour_b, 0, 1), sign_b == 1, target_b, slot_b)
    d_colour_b = jnp.swapaxes(d_colour_b, 0, 1)
    d_log_b = jnp.swapaxes(d_log_b, 0, 1)
    tangents = tuple(flatten(tensor) for tensor in (d_colour_a, d_log_a, d_colour_b, d_log_b))

    def second_pass(pair_item):
        pieces, cotangent = pair_item
        joined, hidden_one, hidden_two, seg_a, seg_b = forward_block(pieces)
        feat_a, dens_a = segment_back(seg_a[2], cotangent[0], cotangent[1], pieces[4], delta_a)
        feat_b, dens_b = segment_back(seg_b[2], cotangent[2], cotangent[3], pieces[5], delta_b)
        d_feature = jnp.concatenate([feat_a, feat_b], 1)
        d_density = jnp.concatenate([dens_a, dens_b], 0)
        return backward_mlp(joined, hidden_one, hidden_two, pieces[6:12], d_feature, d_density)

    grad_in, grad_bin, grad_mid, grad_bmid, grad_feat, grad_dens = lax.map(second_pass, (inputs, tangents))
    return (pixel_a, pixel_b,
            grad_in.reshape(BX, BY, IN, H), grad_bin.reshape(BX, BY, H),
            grad_mid.reshape(BX, BY, H, H), grad_bmid.reshape(BX, BY, H),
            grad_feat.reshape(BX, BY, H, CH), grad_dens.reshape(BX, BY, H))
```

```python
import functools

import jax
import jax.numpy as jnp
from jax import lax
from jax.experimental import pallas as pl
from jax.experimental.pallas import tpu as pltpu
from jax.sharding import PartitionSpec as P

MESH = pl.DeviceIdType.MESH
f32 = jnp.float32
bf16 = jnp.bfloat16

R = 512
S = 4
C = 64
H = 256
K = 64
OPTICAL_DEPTH = 3.0


def dot(a, b):
    return lax.dot_general(a, b, (((1,), (0,)), ((), ())), preferred_element_type=f32)


def dot_t(a, b):
    return lax.dot_general(a, b, (((1,), (1,)), ((), ())), preferred_element_type=f32)


def iota(shape, axis):
    return lax.broadcasted_iota(jnp.int32, shape, axis)


def pack(chunk):
    t = jnp.transpose(chunk).reshape(8, 2, 8, C)
    return jnp.concatenate([t[:, 0].reshape(64, C), t[:, 1].reshape(64, C)], axis=1)


def unpack(tiles):
    n = tiles.shape[0] // 8
    low = tiles[:, :C].reshape(n, 1, 8, C)
    high = tiles[:, C:].reshape(n, 1, 8, C)
    return jnp.concatenate([low, high], axis=1).reshape(16 * n, C)


def softplus(x):
    e = jnp.exp(-jnp.abs(x))
    z = e / (2.0 + e)
    zz = z * z
    tail = 1 / 3 + zz * (1 / 5 + zz * (1 / 7 + zz * (1 / 9 + zz * (1 / 11 + zz * (1 / 13)))))
    return jnp.maximum(x, 0.0) + 2.0 * z * (1.0 + zz * tail)


def one_minus_exp_neg(x):
    small = 1.0 - x * (1 / 8)
    for k in (7, 6, 5, 4, 3, 2):
        small = 1.0 - x * (1 / k) * small
    return jnp.where(x < 0.5, x * small, 1.0 - jnp.exp(-x))


class View:
    def __init__(self, axis, n, delta):
        self.axis = axis
        self.n = n
        self.delta = delta
        self.tiles = R // 16 // n
        self.rays = 16 * self.tiles
        self.per_row = 8 // self.tiles


def far_first(n, t):
    def fold(size, k):
        sign = 1 - 2 * (k % 2)
        return (size // 2 + sign * ((k + 1) // 2)) % size

    if n == 32:
        return 4 * fold(8, t // 4) + fold(4, t % 4)
    return fold(n, t)


def kernel(views, ins, outs, scratch):
    a, b = views
    w = scratch
    nx, ny = a.n, b.n
    me = {"gx": lax.axis_index("gx"), "gy": lax.axis_index("gy")}

    a.at, b.at = 0, 1
    for v, name in ((a, "a"), (b, "b")):
        v.logs, v.colours = w["logs_" + name], w["colours_" + name]
        v.send_aux, v.send_residual = w["send_aux_" + name], w["send_residual_" + name]
        v.aux, v.residuals = w["aux_" + name], w["residuals_" + name]
        v.sems = w["sems_" + name]

    sem = w["in_sem"]
    started = []

    def fetch(src, dst):
        copy = pltpu.make_async_copy(src, dst, sem.at[len(started)])
        copy.start()
        started.append(copy)
        return copy

    def fetch_view(v, name):
        i = me[v.axis]
        got = [
            fetch(ins["count_" + name].at[0], w["count"].at[v.at]),
            fetch(ins["sign_" + name], w["sign"].at[v.at]),
            fetch(ins["slot_" + name], w["slot"].at[v.at]),
        ]
        for s in range(S):
            got.append(
                fetch(
                    ins["samples_" + name].at[0, 0, :, pl.ds(s * R, R)],
                    w["xs"].at[v.at, pl.ds(s * K, K)],
                )
            )
        row = pl.multiple_of((i // v.per_row) * 128, 128)
        v.target = fetch(ins["target_" + name].at[0, :, pl.ds(row, 128)], w["target"].at[v.at])
        return got

    got_a = fetch_view(a, "a")
    got_w = [
        fetch(ins["w_in"].at[0, 0], w["w_in"]),
        fetch(ins["b_in"].at[0], w["b_in"]),
        fetch(ins["w_mid"].at[0, 0], w["w_mid"]),
        fetch(ins["b_mid"].at[0], w["b_mid"]),
        fetch(ins["w_feat"].at[0, 0], w["w_feat"]),
        fetch(ins["w_density"].at[0], w["w_density"]),
    ]
    got_b = fetch_view(b, "b")

    barrier = pltpu.get_barrier_semaphore()
    for v in views:

        def greet(d, carry, v=v):
            peer = lax.rem(me[v.axis] + d, v.n)
            pl.semaphore_signal(barrier, inc=1, device_id={v.axis: peer}, device_id_type=MESH)
            return carry

        lax.fori_loop(1, v.n, greet, 0)

    for copy in got_w:
        copy.wait()
    w["w_in_t"][...] = jnp.transpose(w["w_in"][...].astype(f32)).astype(bf16)
    w["w_mid_t"][...] = jnp.transpose(w["w_mid"][...].astype(f32)).astype(bf16)
    heads = jnp.concatenate(
        [
            w["w_feat"][...].astype(f32),
            w["w_density"][...].astype(f32),
            jnp.zeros((15, H), f32),
        ],
        axis=0,
    )
    w["heads_t"][...] = heads.astype(bf16)
    w["heads"][...] = jnp.transpose(heads).astype(bf16)
    w["bias_in"][...] = jnp.broadcast_to(jnp.transpose(jnp.broadcast_to(w["b_in"][...], (8, H)))[:, :1], (H, 128))
    w["bias_mid"][...] = jnp.broadcast_to(jnp.transpose(jnp.broadcast_to(w["b_mid"][...], (8, H)))[:, :1], (H, 128))
    ones = jnp.where(iota((16, R), 0) == 0, 1.0, 0.0).astype(bf16)

    def forward(v, got):
        at = v.at
        for copy in got:
            copy.wait()
        chosen = (iota((R, R), 0) == w["slot"][at]).astype(bf16)
        counts_signs = jnp.concatenate(
            [w["count"][at].astype(f32), w["sign"][at].astype(f32), jnp.zeros((14, R), f32)], axis=0
        ).astype(bf16)
        counts_signs = dot_t(counts_signs, chosen)
        count, sign = counts_signs[0:1], counts_signs[1:2]
        w["plus"][at] = jnp.broadcast_to(sign, (8, R))
        for g in range(R // 128):
            w["sign_rows"][at, g] = jnp.broadcast_to(sign[:, g * 128 : g * 128 + 128], (8, 128))
        moved = dot_t(w["xs"][at], chosen)
        for s in range(S):
            w["x"][at, s, 0:K] = moved[s * K : s * K + K].astype(bf16)
            w["x"][at, s, K : K + 16] = ones
            w["h1"][at, s, H : H + 16] = ones
        bias_in = jnp.concatenate([w["bias_in"][...]] * (R // 128), axis=1)
        bias_mid = jnp.concatenate([w["bias_mid"][...]] * (R // 128), axis=1)

        def slot(s, carry):
            one = dot(w["w_in_t"][...], w["x"][at, s, 0:K]) + bias_in
            one = jnp.maximum(one, 0.0).astype(bf16)
            w["h1"][at, s, 0:H] = one
            two = dot(w["w_mid_t"][...], one) + bias_mid
            two = jnp.maximum(two, 0.0).astype(bf16)
            w["h2"][at, s] = two
            fd = dot(w["heads_t"][...], two)
            w["feature"][at, s] = fd[0:C]
            w["density"][at, s] = fd[C : C + 8]
            return carry

        lax.fori_loop(0, S, slot, 0)

        density = jnp.concatenate([w["density"][at, s, 0:1] for s in range(S)], axis=0)
        masked = (iota((S, R), 0).astype(f32) < count).astype(f32)
        optical = v.delta * softplus(density) * masked
        rows = [optical[s : s + 1] for s in range(S)]
        upto = [rows[0]]
        for s in range(1, S):
            upto.append(upto[-1] + rows[s])
        total = upto[-1]
        plus = sign > 0.5
        before = jnp.concatenate(
            [jnp.where(plus, upto[s] - rows[s], total - upto[s]) for s in range(S)], axis=0
        )
        weight = jnp.exp(-before) * one_minus_exp_neg(optical)
        w["weight"][at] = weight
        w["behind_slot"][at] = jnp.exp(-(before + optical))
        w["slope"][at] = v.delta * masked * lax.logistic(density)
        for g in range(R // 128):
            lanes = slice(g * 128, g * 128 + 128)
            w["send_log"][at, g] = -total[:, lanes]
            colour = weight[0:1, lanes] * w["feature"][at, 0, :, lanes]
            for s in range(1, S):
                colour = colour + weight[s : s + 1, lanes] * w["feature"][at, s, :, lanes]
            w["send_colour"][at, g * 64 : g * 64 + 64] = pack(colour)

    def each_peer(v, fn):
        def body(t, carry):
            fn(lax.rem(me[v.axis] + far_first(v.n, t), v.n))
            return carry

        lax.fori_loop(0, v.n - 1, body, 0)

    def colour_copies(v, peer, mine):
        rows = 8 * v.tiles
        return (
            pltpu.make_async_remote_copy(
                src_ref=w["send_log"].at[v.at, peer // v.per_row],
                dst_ref=v.logs.at[mine],
                send_sem=v.sems.at[0, peer],
                recv_sem=v.sems.at[1, mine],
                device_id={v.axis: peer},
                device_id_type=MESH,
            ),
            pltpu.make_async_remote_copy(
                src_ref=w["send_colour"].at[v.at, pl.ds(pl.multiple_of(peer * rows, 8), rows)],
                dst_ref=v.colours.at[mine],
                send_sem=v.sems.at[2, peer],
                recv_sem=v.sems.at[3, mine],
                device_id={v.axis: peer},
                device_id_type=MESH,
            ),
        )

    def back_copies(v, peer, mine):
        return (
            pltpu.make_async_remote_copy(
                src_ref=v.send_aux.at[peer],
                dst_ref=v.aux.at[mine],
                send_sem=v.sems.at[4, peer],
                recv_sem=v.sems.at[5, mine],
                device_id={v.axis: peer},
                device_id_type=MESH,
            ),
            pltpu.make_async_remote_copy(
                src_ref=v.send_residual,
                dst_ref=v.residuals.at[mine],
                send_sem=v.sems.at[6, peer],
                recv_sem=v.sems.at[7, mine],
                device_id={v.axis: peer},
                device_id_type=MESH,
            ),
        )

    def send(v, copies):
        def start(peer):
            for copy in copies(v, peer, me[v.axis]):
                copy.start()

        each_peer(v, start)

    def received(v, copies):
        def wait(peer):
            for copy in copies(v, me[v.axis], peer):
                copy.wait_recv()

        each_peer(v, wait)

    def sent(v, copies):
        def wait(peer):
            for copy in copies(v, peer, me[v.axis]):
                copy.wait_send()

        each_peer(v, wait)

    def scan(x, n, back):
        step = 1
        while step < n:
            x = x + pltpu.roll(x, 128 - step if back else step, 1)
            step *= 2
        return x

    def own(v, name):
        at, i, n = v.at, me[v.axis], v.n
        rows = 8 * v.tiles
        part = pl.multiple_of(lax.rem(i, v.per_row) * v.rays, 16)
        v.target.wait()
        w["tile"][...] = pack(w["target"][at])
        target = w["tile"][pl.ds(pl.multiple_of(lax.rem(i, v.per_row) * rows, 8), rows)]
        v.logs[i] = w["send_log"][at, i // v.per_row]
        v.colours[i] = w["send_colour"][at, pl.ds(pl.multiple_of(i * rows, 8), rows)]
        received(v, colour_copies)
        logs = jnp.concatenate(
            [v.logs[...].reshape(n, 128), w["sign_rows"][at, i // v.per_row], jnp.zeros((120 - n, 128), f32)],
            axis=0,
        )
        w["turn"][...] = jnp.transpose(logs)
        mine = w["turn"][pl.ds(part, v.rays)]
        lane = iota((v.rays, 128), 1)
        plus = mine[:, n : n + 1] > 0.5
        mine = jnp.where(lane < n, mine, 0.0)

        def beyond(x, ahead):
            low = pltpu.roll(scan(x, n, False), 1, 1)
            high = pltpu.roll(scan(x, n, True), 127, 1)
            return jnp.where(plus, low, high) if ahead else jnp.where(plus, high, low)

        front = jnp.where(lane < n, jnp.exp(beyond(mine, True)), 0.0)
        half = iota((8, 128), 1) < C
        lane8 = iota((8, 128), 1)
        seen = []
        for t in range(v.tiles):
            low, high = front[16 * t : 16 * t + 8], front[16 * t + 8 : 16 * t + 16]
            pixel = None
            for k in range(n):
                part_k = jnp.where(half, low[:, k : k + 1], high[:, k : k + 1])
                part_k = part_k * v.colours[k, 8 * t : 8 * t + 8]
                pixel = part_k if pixel is None else pixel + part_k
            residual = pixel - target[8 * t : 8 * t + 8]
            v.send_residual[8 * t : 8 * t + 8] = residual
            w["pixel_" + name][8 * t : 8 * t + 8] = pixel
            seen_low = jnp.zeros((8, 128), f32)
            seen_high = jnp.zeros((8, 128), f32)
            for k in range(n):
                product = residual * v.colours[k, 8 * t : 8 * t + 8]
                at_low = jnp.sum(jnp.where(half, product, 0.0), axis=1, keepdims=True)
                at_high = jnp.sum(jnp.where(half, 0.0, product), axis=1, keepdims=True)
                seen_low = jnp.where(lane8 == k, at_low, seen_low)
                seen_high = jnp.where(lane8 == k, at_high, seen_high)
            seen += [seen_low, seen_high]
        d_log = jnp.where(lane < n, beyond(front * jnp.concatenate(seen, axis=0), False), 0.0)
        w["turn"][...] = jnp.zeros((128, 128), f32)
        w["turn"][pl.ds(part, v.rays)] = front + pltpu.roll(d_log, 64, 1)
        turned = jnp.transpose(w["turn"][...])
        v.send_aux[...] = (turned[0:n] + pltpu.roll(turned[64 : 64 + n], 64, 1)).reshape(n, 1, 128)
        v.aux[i] = v.send_aux[i]
        v.residuals[i] = v.send_residual[...]

    def backward(v, first):
        at, n = v.at, v.n
        received(v, back_copies)
        aux = v.aux[...].reshape(n, 128)
        group = iota((n, 128), 1) // v.rays
        place = iota((n, 128), 0) % v.per_row
        fronts = jnp.where(group == place, aux, 0.0)
        logs = jnp.where(group == (place + 4 // v.tiles) % v.per_row, aux, 0.0)
        tiles = v.residuals[...].reshape(R // 2, 128)
        d_log = []
        for g in range(R // 128):
            part = slice(g * v.per_row, (g + 1) * v.per_row)
            front = jnp.sum(fronts[part], axis=0, keepdims=True)
            d_log.append(pltpu.roll(jnp.broadcast_to(jnp.sum(logs[part], axis=0, keepdims=True), (8, 128)), 64, 1)[0:1])
            residual = jnp.transpose(unpack(tiles[g * 64 : g * 64 + 64]))
            w["d_colour"][:, g * 128 : g * 128 + 128] = front * residual
        d_log = jnp.concatenate(d_log, axis=1)
        weight = w["weight"][at]
        d_weight = []
        for s in range(S):
            d_weight.append(jnp.sum(w["feature"][at, s] * w["d_colour"][...], axis=0, keepdims=True))
            w["d_heads"][s, 0:C] = (weight[s : s + 1] * w["d_colour"][...]).astype(bf16)
        product = [d_weight[s] * weight[s : s + 1] for s in range(S)]
        upto = [product[0]]
        for s in range(1, S):
            upto.append(upto[-1] + product[s])
        plus = w["plus"][at, 0:1] > 0.5
        for s in range(S):
            later = jnp.where(plus, upto[-1] - upto[s], upto[s] - product[s])
            d_optical = w["behind_slot"][at, s : s + 1] * d_weight[s] - d_log - later
            d_density = d_optical * w["slope"][at, s : s + 1]
            w["d_heads"][s, C : C + 16] = jnp.where(iota((16, R), 0) == 0, d_density, 0.0).astype(bf16)

        def slot(s, carry):
            d_heads = w["d_heads"][s]
            two = w["h2"][at, s]
            one = w["h1"][at, s]
            d_two = dot(w["heads"][...], d_heads)
            d_two = jnp.where(two > 0, d_two.astype(bf16), jnp.zeros((), bf16))
            d_one = dot(w["w_mid"][...], d_two)
            d_one = jnp.where(one[0:H] > 0, d_one.astype(bf16), jnp.zeros((), bf16))
            w["g_heads"][...] += dot_t(d_heads, two)
            w["g_mid"][...] += dot_t(one, d_two)
            w["g_in"][...] += dot_t(w["x"][at, s], d_one)
            return carry

        lax.fori_loop(0, S, slot, 0)

    forward(a, got_a)
    pl.semaphore_wait(barrier, nx + ny - 2)
    send(a, colour_copies)
    w["g_heads"][...] = jnp.zeros_like(w["g_heads"])
    w["g_mid"][...] = jnp.zeros_like(w["g_mid"])
    w["g_in"][...] = jnp.zeros_like(w["g_in"])
    forward(b, got_b)
    send(b, colour_copies)
    own(b, "b")
    send(b, back_copies)
    own(a, "a")
    send(a, back_copies)
    backward(b, True)
    backward(a, False)
    outs["mid"][...] = w["g_mid"][...]
    outs["in"][...] = w["g_in"][...]
    outs["heads"][...] = w["g_heads"][...]
    outs["pixel_a"][...] = w["pixel_a"][...]
    outs["pixel_b"][...] = w["pixel_b"][...]
    for v in views:
        sent(v, colour_copies)
        sent(v, back_copies)


def finish(mid, first, heads, pixel_a, pixel_b, o_pa, o_pb, o_win, o_bin, o_wmid, o_bmid, o_wfeat, o_wden):
    o_wmid[0, 0] = mid[0:H]
    o_bmid[0] = mid[H : H + 1]
    o_win[0, 0] = first[0:K]
    o_bin[0] = first[K : K + 1]
    o_wfeat[0, 0] = heads[0:C]
    o_wden[0] = heads[C : C + 1]
    o_pa[0] = unpack(pixel_a[...])
    o_pb[0] = jnp.transpose(unpack(pixel_b[...]))


NAMES = (
    ("samples_a", "samples_b", "count_a", "count_b", "sign_a", "sign_b", "slot_a", "slot_b")
    + ("target_a", "target_b", "w_in", "b_in", "w_mid", "b_mid", "w_feat", "w_density")
)


def on_device(nx, ny, *args):
    names = NAMES
    out_names = ["mid", "in", "heads", "pixel_a", "pixel_b"]
    ta, tb = R // 16 // nx, R // 16 // ny
    args = args[:14] + (jnp.swapaxes(args[14], 2, 3),) + args[15:]
    vm = pltpu.VMEM
    scratch = {
        "in_sem": pltpu.SemaphoreType.DMA((32,)),
        "count": vm((2, 1, R), jnp.int32),
        "sign": vm((2, 1, R), jnp.int32),
        "slot": vm((2, 1, R), jnp.int32),
        "xs": vm((2, S * K, R), bf16),
        "target": vm((2, C, 128), f32),
        "w_in": vm((K, H), bf16),
        "b_in": vm((1, H), f32),
        "w_mid": vm((H, H), bf16),
        "b_mid": vm((1, H), f32),
        "w_feat": vm((C, H), bf16),
        "w_density": vm((1, H), bf16),
        "w_in_t": vm((H, K), bf16),
        "w_mid_t": vm((H, H), bf16),
        "heads_t": vm((C + 16, H), bf16),
        "heads": vm((H, C + 16), bf16),
        "bias_in": vm((H, 128), f32),
        "bias_mid": vm((H, 128), f32),
        "plus": vm((2, 8, R), f32),
        "sign_rows": vm((2, R // 128, 8, 128), f32),
        "x": vm((2, S, K + 16, R), bf16),
        "h1": vm((2, S, H + 16, R), bf16),
        "h2": vm((2, S, H, R), bf16),
        "feature": vm((2, S, C, R), f32),
        "density": vm((2, S, 8, R), f32),
        "weight": vm((2, S, R), f32),
        "behind_slot": vm((2, S, R), f32),
        "slope": vm((2, S, R), f32),
        "send_log": vm((2, R // 128, 1, 128), f32),
        "send_colour": vm((2, R // 2, 128), f32),
        "tile": vm((64, 128), f32),
        "turn": vm((128, 128), f32),
        "d_colour": vm((C, R), f32),
        "d_heads": vm((S, C + 16, R), bf16),
        "g_mid": vm((H + 16, H), f32),
        "g_in": vm((K + 16, H), f32),
        "g_heads": vm((C + 16, H), f32),
    }
    for name, n, t in (("a", nx, ta), ("b", ny, tb)):
        scratch["pixel_" + name] = vm((8 * t, 128), f32)
        scratch["logs_" + name] = vm((n, 1, 128), f32)
        scratch["colours_" + name] = vm((n, 8 * t, 128), f32)
        scratch["send_aux_" + name] = vm((n, 1, 128), f32)
        scratch["send_residual_" + name] = vm((8 * t, 128), f32)
        scratch["aux_" + name] = vm((n, 1, 128), f32)
        scratch["residuals_" + name] = vm((n, 8 * t, 128), f32)
        scratch["sems_" + name] = pltpu.SemaphoreType.DMA((8, n))
    keys = list(scratch)
    n_in, n_out = len(names), len(out_names)

    def body(*refs):
        ins = dict(zip(names, refs[:n_in]))
        outs = dict(zip(out_names, refs[n_in : n_in + n_out]))
        views = (
            View("gx", nx, OPTICAL_DEPTH / (nx * S)),
            View("gy", ny, OPTICAL_DEPTH / (ny * S)),
        )
        kernel(views, ins, outs, dict(zip(keys, refs[n_in + n_out :])))

    vmem = pl.BlockSpec(memory_space=pltpu.VMEM)
    middle = pl.pallas_call(
        body,
        name="step",
        out_shape=(
            jax.ShapeDtypeStruct((H + 16, H), f32),
            jax.ShapeDtypeStruct((K + 16, H), f32),
            jax.ShapeDtypeStruct((C + 16, H), f32),
            jax.ShapeDtypeStruct((8 * ta, 128), f32),
            jax.ShapeDtypeStruct((8 * tb, 128), f32),
        ),
        in_specs=[pl.BlockSpec(memory_space=pl.ANY)] * n_in,
        out_specs=(vmem,) * n_out,
        scratch_shapes=[scratch[key] for key in keys],
        compiler_params=pltpu.CompilerParams(collective_id=0, has_side_effects=True),
    )(*args)
    done = pl.pallas_call(
        finish,
        name="finish",
        out_shape=(
            jax.ShapeDtypeStruct((1, R // nx, C), f32),
            jax.ShapeDtypeStruct((1, C, R // ny), f32),
            jax.ShapeDtypeStruct((1, 1, K, H), f32),
            jax.ShapeDtypeStruct((1, 1, H), f32),
            jax.ShapeDtypeStruct((1, 1, H, H), f32),
            jax.ShapeDtypeStruct((1, 1, H), f32),
            jax.ShapeDtypeStruct((1, 1, C, H), f32),
            jax.ShapeDtypeStruct((1, 1, H), f32),
        ),
        in_specs=[vmem] * n_out,
        out_specs=(vmem,) * 8,
    )(*middle)
    pixel_a, pixel_b, g_in, g_bin, g_mid, g_bmid, g_feat, g_density = done
    return jnp.swapaxes(pixel_a, 1, 2), pixel_b, g_in, g_bin, g_mid, g_bmid, jnp.swapaxes(g_feat, 2, 3), g_density


def solution(mesh):
    block = P("gx", "gy", None, None)
    vector = P("gx", "gy", None)
    in_specs = (block, block, vector, vector)
    in_specs += (P("gy", None), P("gx", None), P("gy", None), P("gx", None))
    in_specs += (P("gy", None, None), P("gx", None, None))
    in_specs += (block, vector, block, vector, block, vector)
    out_specs = (P("gy", None, "gx"), P("gx", None, "gy"))
    out_specs += (block, vector, block, vector, block, vector)
    return jax.shard_map(
        functools.partial(on_device, mesh.shape["gx"], mesh.shape["gy"]),
        mesh=mesh,
        in_specs=in_specs,
        out_specs=out_specs,
        check_vma=False,
    )
```

```python
import functools
from types import SimpleNamespace

import jax
import jax.numpy as jnp
from jax import lax
from jax.experimental import pallas as pl
from jax.experimental.pallas import tpu as pltpu
from jax.sharding import PartitionSpec as P

MESH = pl.DeviceIdType.MESH
f32 = jnp.float32
bf16 = jnp.bfloat16

R = 512
S = 4
C = 64
H = 256
K = 64
OPTICAL_DEPTH = 3.0


def dot(a, b):
    return lax.dot_general(a, b, (((1,), (0,)), ((), ())), preferred_element_type=f32)


def dot_t(a, b):
    return lax.dot_general(a, b, (((1,), (1,)), ((), ())), preferred_element_type=f32)


def iota(shape, axis):
    return lax.broadcasted_iota(jnp.int32, shape, axis)


def pack(chunk):
    t = jnp.transpose(chunk).reshape(8, 2, 8, C)
    return jnp.concatenate([t[:, 0].reshape(64, C), t[:, 1].reshape(64, C)], axis=1)


def unpack(tiles):
    n = tiles.shape[0] // 8
    low = tiles[:, :C].reshape(n, 1, 8, C)
    high = tiles[:, C:].reshape(n, 1, 8, C)
    return jnp.concatenate([low, high], axis=1).reshape(16 * n, C)


def softplus(x):
    e = jnp.exp(-jnp.abs(x))
    z = e / (2.0 + e)
    zz = z * z
    tail = 1 / 3 + zz * (1 / 5 + zz * (1 / 7 + zz * (1 / 9 + zz * (1 / 11 + zz * (1 / 13)))))
    return jnp.maximum(x, 0.0) + 2.0 * z * (1.0 + zz * tail)


def one_minus_exp_neg(x):
    small = 1.0 - x * (1 / 8)
    for k in (7, 6, 5, 4, 3, 2):
        small = 1.0 - x * (1 / k) * small
    return jnp.where(x < 0.5, x * small, 1.0 - jnp.exp(-x))


class View:
    def __init__(self, axis, n, at):
        self.axis = axis
        self.n = n
        self.at = at
        self.delta = OPTICAL_DEPTH / (n * S)
        self.tiles = R // 16 // n
        self.rays = 16 * self.tiles
        self.per_row = 8 // self.tiles


def ring(i, size):
    return [lax.rem(i + o, size) for o in range(size)]


def line_peers(i, n):
    if n == 32:
        sizes = (8, 4)
    elif n == 8:
        sizes = (4, 2)
    else:
        sizes = (n, 1)
    slow, fast = ring(i // sizes[1], sizes[0]), ring(lax.rem(i, sizes[1]), sizes[1])
    hops = {}
    for p in range(sizes[0]):
        for q in range(sizes[1]):
            hops[p, q] = min(p, sizes[0] - p) + min(q, sizes[1] - q) * (1.0 if n == 32 else 0.1)
    order = sorted(hops, key=lambda pq: -hops[pq])[:-1]
    return [slow[p] * sizes[1] + fast[q] for p, q in order]


def kernel(views, ins, outs, w):
    a, b = views

    for v in views:
        v.i = lax.axis_index(v.axis)
        v.peers = line_peers(v.i, v.n)

    sem = w.in_sem
    started = []

    def fetch(src, dst):
        copy = pltpu.make_async_copy(src, dst, sem.at[len(started)])
        copy.start()
        started.append(copy)
        return copy

    def fetch_view(v):
        row = pl.multiple_of((v.i // v.per_row) * 128, 128)
        got = [
            fetch(v.count.at[0], w.count.at[v.at]),
            fetch(v.sign, w.sign.at[v.at]),
            fetch(v.slot, w.slot.at[v.at]),
        ]
        for s in range(S):
            part = v.samples.at[0, 0, :, pl.ds(s * R, R)]
            got.append(fetch(part, w.xs.at[v.at, pl.ds(s * K, K)]))
        v.target_in = fetch(v.target.at[0, :, pl.ds(row, 128)], w.target.at[v.at])
        return got

    got_a = fetch_view(a)
    got_w = [
        fetch(ins.w_in.at[0, 0], w.w_in),
        fetch(ins.b_in.at[0], w.b_in),
        fetch(ins.w_mid.at[0, 0], w.w_mid),
        fetch(ins.b_mid.at[0], w.b_mid),
        fetch(ins.w_feat.at[0, 0], w.w_feat),
        fetch(ins.w_density.at[0], w.w_density),
    ]
    got_b = fetch_view(b)

    barrier = pltpu.get_barrier_semaphore()
    for v in views:
        for peer in v.peers:
            pl.semaphore_signal(barrier, inc=1, device_id={v.axis: peer}, device_id_type=MESH)

    for copy in got_w:
        copy.wait()
    w.w_in_t[...] = jnp.transpose(w.w_in[...].astype(f32)).astype(bf16)
    w.w_mid_t[...] = jnp.transpose(w.w_mid[...].astype(f32)).astype(bf16)
    heads = jnp.concatenate(
        [
            w.w_feat[...].astype(f32),
            w.w_density[...].astype(f32),
            jnp.zeros((15, H), f32),
        ],
        axis=0,
    )
    w.heads_t[...] = heads.astype(bf16)
    w.heads[...] = jnp.transpose(heads).astype(bf16)
    w.bias_in[...] = jnp.broadcast_to(jnp.transpose(jnp.broadcast_to(w.b_in[...], (8, H)))[:, :1], (H, 128))
    w.bias_mid[...] = jnp.broadcast_to(jnp.transpose(jnp.broadcast_to(w.b_mid[...], (8, H)))[:, :1], (H, 128))
    ones = jnp.where(iota((16, R), 0) == 0, 1.0, 0.0).astype(bf16)

    def forward(v, got):
        at = v.at
        for copy in got:
            copy.wait()
        chosen = (iota((R, R), 0) == w.slot[at]).astype(bf16)
        counts_signs = jnp.concatenate(
            [w.count[at].astype(f32), w.sign[at].astype(f32), jnp.zeros((14, R), f32)], axis=0
        ).astype(bf16)
        counts_signs = dot_t(counts_signs, chosen)
        count, sign = counts_signs[0:1], counts_signs[1:2]
        w.plus[at] = jnp.broadcast_to(sign, (8, R))
        for g in range(R // 128):
            w.sign_rows[at, g] = jnp.broadcast_to(sign[:, g * 128 : g * 128 + 128], (8, 128))
        moved = dot_t(w.xs[at], chosen)
        for s in range(S):
            w.x[at, s, 0:K] = moved[s * K : s * K + K].astype(bf16)
            w.x[at, s, K : K + 16] = ones
            w.h1[at, s, H : H + 16] = ones
        bias_in = jnp.concatenate([w.bias_in[...]] * (R // 128), axis=1)
        bias_mid = jnp.concatenate([w.bias_mid[...]] * (R // 128), axis=1)

        def slot(s, carry):
            one = dot(w.w_in_t[...], w.x[at, s, 0:K]) + bias_in
            one = jnp.maximum(one, 0.0).astype(bf16)
            w.h1[at, s, 0:H] = one
            two = dot(w.w_mid_t[...], one) + bias_mid
            two = jnp.maximum(two, 0.0).astype(bf16)
            w.h2[at, s] = two
            fd = dot(w.heads_t[...], two)
            w.feature[at, s] = fd[0:C]
            w.density[at, s] = fd[C : C + 8]
            return carry

        lax.fori_loop(0, S, slot, 0)

        density = jnp.concatenate([w.density[at, s, 0:1] for s in range(S)], axis=0)
        masked = (iota((S, R), 0).astype(f32) < count).astype(f32)
        optical = v.delta * softplus(density) * masked
        rows = [optical[s : s + 1] for s in range(S)]
        upto = [rows[0]]
        for s in range(1, S):
            upto.append(upto[-1] + rows[s])
        total = upto[-1]
        plus = sign > 0.5
        before = jnp.concatenate(
            [jnp.where(plus, upto[s] - rows[s], total - upto[s]) for s in range(S)], axis=0
        )
        weight = jnp.exp(-before) * one_minus_exp_neg(optical)
        w.weight[at] = weight
        w.behind_slot[at] = jnp.exp(-(before + optical))
        w.slope[at] = v.delta * masked * lax.logistic(density)
        for g in range(R // 128):
            lanes = slice(g * 128, g * 128 + 128)
            w.send_log[at, g] = -total[:, lanes]
            colour = weight[0:1, lanes] * w.feature[at, 0, :, lanes]
            for s in range(1, S):
                colour = colour + weight[s : s + 1, lanes] * w.feature[at, s, :, lanes]
            w.send_colour[at, g * 64 : g * 64 + 64] = pack(colour)

    def start(v, src, dst, k, peer):
        pltpu.make_async_remote_copy(
            src_ref=src,
            dst_ref=dst.at[v.i],
            send_sem=v.sems.at[0, k],
            recv_sem=v.sems.at[1, k],
            device_id={v.axis: peer},
            device_id_type=MESH,
        ).start()

    def wait(v, way, dst, k):
        every = dst.at[pl.ds(0, v.n - 1)]
        pltpu.make_async_copy(every, every, v.sems.at[way, k]).wait()

    def send_segments(v):
        rows = 8 * v.tiles
        for peer in v.peers:
            start(v, w.send_log.at[v.at, peer // v.per_row], v.logs, 0, peer)
            tiles = pl.ds(pl.multiple_of(peer * rows, 8), rows)
            start(v, w.send_colour.at[v.at, tiles], v.colours, 1, peer)

    def send_back(v):
        for peer in v.peers:
            start(v, v.send_aux.at[peer], v.aux, 2, peer)
            start(v, v.send_residual, v.residuals, 3, peer)

    def scan(x, n, back):
        step = 1
        while step < n:
            x = x + pltpu.roll(x, 128 - step if back else step, 1)
            step *= 2
        return x

    def own(v):
        at, i, n = v.at, v.i, v.n
        rows = 8 * v.tiles
        part = pl.multiple_of(lax.rem(i, v.per_row) * v.rays, 16)
        v.target_in.wait()
        w.tile[...] = pack(w.target[at])
        target = w.tile[pl.ds(pl.multiple_of(lax.rem(i, v.per_row) * rows, 8), rows)]
        v.logs[i] = w.send_log[at, i // v.per_row]
        v.colours[i] = w.send_colour[at, pl.ds(pl.multiple_of(i * rows, 8), rows)]
        wait(v, 1, v.logs, 0)
        wait(v, 1, v.colours, 1)
        logs = jnp.concatenate(
            [v.logs[...].reshape(n, 128), w.sign_rows[at, i // v.per_row], jnp.zeros((120 - n, 128), f32)],
            axis=0,
        )
        w.turn[...] = jnp.transpose(logs)
        mine = w.turn[pl.ds(part, v.rays)]
        lane = iota((v.rays, 128), 1)
        plus = mine[:, n : n + 1] > 0.5
        mine = jnp.where(lane < n, mine, 0.0)

        def beyond(x, ahead):
            low = pltpu.roll(scan(x, n, False), 1, 1)
            high = pltpu.roll(scan(x, n, True), 127, 1)
            return jnp.where(plus, low, high) if ahead else jnp.where(plus, high, low)

        front = jnp.where(lane < n, jnp.exp(beyond(mine, True)), 0.0)
        half = iota((8, 128), 1) < C
        lane8 = iota((8, 128), 1)
        seen = []
        for t in range(v.tiles):
            low, high = front[16 * t : 16 * t + 8], front[16 * t + 8 : 16 * t + 16]
            pixel = None
            for k in range(n):
                part_k = jnp.where(half, low[:, k : k + 1], high[:, k : k + 1])
                part_k = part_k * v.colours[k, 8 * t : 8 * t + 8]
                pixel = part_k if pixel is None else pixel + part_k
            residual = pixel - target[8 * t : 8 * t + 8]
            v.send_residual[8 * t : 8 * t + 8] = residual
            v.pixel[8 * t : 8 * t + 8] = pixel
            seen_low = jnp.zeros((8, 128), f32)
            seen_high = jnp.zeros((8, 128), f32)
            for k in range(n):
                product = residual * v.colours[k, 8 * t : 8 * t + 8]
                at_low = jnp.sum(jnp.where(half, product, 0.0), axis=1, keepdims=True)
                at_high = jnp.sum(jnp.where(half, 0.0, product), axis=1, keepdims=True)
                seen_low = jnp.where(lane8 == k, at_low, seen_low)
                seen_high = jnp.where(lane8 == k, at_high, seen_high)
            seen += [seen_low, seen_high]
        d_log = jnp.where(lane < n, beyond(front * jnp.concatenate(seen, axis=0), False), 0.0)
        w.turn[...] = jnp.zeros((128, 128), f32)
        w.turn[pl.ds(part, v.rays)] = front + pltpu.roll(d_log, 64, 1)
        turned = jnp.transpose(w.turn[...])
        v.send_aux[...] = (turned[0:n] + pltpu.roll(turned[64 : 64 + n], 64, 1)).reshape(n, 1, 128)
        v.aux[i] = v.send_aux[i]
        v.residuals[i] = v.send_residual[...]

    def backward(v):
        at, n = v.at, v.n
        wait(v, 1, v.aux, 2)
        wait(v, 1, v.residuals, 3)
        aux = v.aux[...].reshape(n, 128)
        group = iota((n, 128), 1) // v.rays
        place = iota((n, 128), 0) % v.per_row
        fronts = jnp.where(group == place, aux, 0.0)
        logs = jnp.where(group == (place + 4 // v.tiles) % v.per_row, aux, 0.0)
        tiles = v.residuals[...].reshape(R // 2, 128)
        d_log = []
        for g in range(R // 128):
            part = slice(g * v.per_row, (g + 1) * v.per_row)
            front = jnp.sum(fronts[part], axis=0, keepdims=True)
            d_log.append(pltpu.roll(jnp.broadcast_to(jnp.sum(logs[part], axis=0, keepdims=True), (8, 128)), 64, 1)[0:1])
            residual = jnp.transpose(unpack(tiles[g * 64 : g * 64 + 64]))
            w.d_colour[:, g * 128 : g * 128 + 128] = front * residual
        d_log = jnp.concatenate(d_log, axis=1)
        weight = w.weight[at]
        d_weight = []
        for s in range(S):
            d_weight.append(jnp.sum(w.feature[at, s] * w.d_colour[...], axis=0, keepdims=True))
            w.d_heads[s, 0:C] = (weight[s : s + 1] * w.d_colour[...]).astype(bf16)
        product = [d_weight[s] * weight[s : s + 1] for s in range(S)]
        upto = [product[0]]
        for s in range(1, S):
            upto.append(upto[-1] + product[s])
        plus = w.plus[at, 0:1] > 0.5
        for s in range(S):
            later = jnp.where(plus, upto[-1] - upto[s], upto[s] - product[s])
            d_optical = w.behind_slot[at, s : s + 1] * d_weight[s] - d_log - later
            d_density = d_optical * w.slope[at, s : s + 1]
            w.d_heads[s, C : C + 16] = jnp.where(iota((16, R), 0) == 0, d_density, 0.0).astype(bf16)

        def slot(s, carry):
            d_heads = w.d_heads[s]
            two = w.h2[at, s]
            one = w.h1[at, s]
            d_two = dot(w.heads[...], d_heads)
            d_two = jnp.where(two > 0, d_two.astype(bf16), jnp.zeros((), bf16))
            d_one = dot(w.w_mid[...], d_two)
            d_one = jnp.where(one[0:H] > 0, d_one.astype(bf16), jnp.zeros((), bf16))
            w.g_heads[...] += dot_t(d_heads, two)
            w.g_mid[...] += dot_t(one, d_two)
            w.g_in[...] += dot_t(w.x[at, s], d_one)
            return carry

        lax.fori_loop(0, S, slot, 0)

    forward(a, got_a)
    pl.semaphore_wait(barrier, a.n + b.n - 2)
    send_segments(a)
    w.g_heads[...] = jnp.zeros_like(w.g_heads)
    w.g_mid[...] = jnp.zeros_like(w.g_mid)
    w.g_in[...] = jnp.zeros_like(w.g_in)
    forward(b, got_b)
    send_segments(b)
    own(b)
    send_back(b)
    own(a)
    send_back(a)
    backward(b)
    backward(a)
    outs.mid[...] = w.g_mid[...]
    outs.first[...] = w.g_in[...]
    outs.heads[...] = w.g_heads[...]
    outs.pixel_a[...] = a.pixel[...]
    outs.pixel_b[...] = b.pixel[...]
    for v in views:
        for k, dst in enumerate((v.logs, v.colours, v.aux, v.residuals)):
            wait(v, 0, dst, k)


def finish(mid, first, heads, pixel_a, pixel_b, o_pa, o_pb, o_win, o_bin, o_wmid, o_bmid, o_wfeat, o_wden):
    o_wmid[0, 0] = mid[0:H]
    o_bmid[0] = mid[H : H + 1]
    o_win[0, 0] = first[0:K]
    o_bin[0] = first[K : K + 1]
    o_wfeat[0, 0] = heads[0:C]
    o_wden[0] = heads[C : C + 1]
    o_pa[0] = unpack(pixel_a[...])
    o_pb[0] = jnp.transpose(unpack(pixel_b[...]))


def on_device(nx, ny, *args):
    ta, tb = R // 16 // nx, R // 16 // ny
    args = args[:14] + (jnp.swapaxes(args[14], 2, 3),) + args[15:]
    vm = pltpu.VMEM
    scratch = dict(
        in_sem=pltpu.SemaphoreType.DMA((32,)),
        count=vm((2, 1, R), jnp.int32),
        sign=vm((2, 1, R), jnp.int32),
        slot=vm((2, 1, R), jnp.int32),
        xs=vm((2, S * K, R), bf16),
        target=vm((2, C, 128), f32),
        w_in=vm((K, H), bf16),
        b_in=vm((1, H), f32),
        w_mid=vm((H, H), bf16),
        b_mid=vm((1, H), f32),
        w_feat=vm((C, H), bf16),
        w_density=vm((1, H), bf16),
        w_in_t=vm((H, K), bf16),
        w_mid_t=vm((H, H), bf16),
        heads_t=vm((C + 16, H), bf16),
        heads=vm((H, C + 16), bf16),
        bias_in=vm((H, 128), f32),
        bias_mid=vm((H, 128), f32),
        plus=vm((2, 8, R), f32),
        sign_rows=vm((2, R // 128, 8, 128), f32),
        x=vm((2, S, K + 16, R), bf16),
        h1=vm((2, S, H + 16, R), bf16),
        h2=vm((2, S, H, R), bf16),
        feature=vm((2, S, C, R), f32),
        density=vm((2, S, 8, R), f32),
        weight=vm((2, S, R), f32),
        behind_slot=vm((2, S, R), f32),
        slope=vm((2, S, R), f32),
        send_log=vm((2, R // 128, 1, 128), f32),
        send_colour=vm((2, R // 2, 128), f32),
        tile=vm((64, 128), f32),
        turn=vm((128, 128), f32),
        d_colour=vm((C, R), f32),
        d_heads=vm((S, C + 16, R), bf16),
        g_mid=vm((H + 16, H), f32),
        g_in=vm((K + 16, H), f32),
        g_heads=vm((C + 16, H), f32),
    )
    def line_buffers(n, tiles):
        return dict(
            pixel=vm((8 * tiles, 128), f32),
            logs=vm((n, 1, 128), f32),
            colours=vm((n, 8 * tiles, 128), f32),
            send_aux=vm((n, 1, 128), f32),
            send_residual=vm((8 * tiles, 128), f32),
            aux=vm((n, 1, 128), f32),
            residuals=vm((n, 8 * tiles, 128), f32),
            sems=pltpu.SemaphoreType.DMA((2, 4)),
        )

    buffers = (scratch, line_buffers(nx, ta), line_buffers(ny, tb))
    shapes = [shape for group in buffers for shape in group.values()]
    n_in, n_out = len(args), 5

    def body(*refs):
        views = (View("gx", nx, 0), View("gy", ny, 1))
        (
            *by_view,
            w_in,
            b_in,
            w_mid,
            b_mid,
            w_feat,
            w_density,
        ) = refs[:n_in]
        for v in views:
            v.samples, v.count, v.sign, v.slot, v.target = by_view[v.at :: 2]
        ins = SimpleNamespace(w_in=w_in, b_in=b_in, w_mid=w_mid, b_mid=b_mid, w_feat=w_feat, w_density=w_density)
        mid, first, heads, pixel_a, pixel_b = refs[n_in : n_in + n_out]
        outs = SimpleNamespace(mid=mid, first=first, heads=heads, pixel_a=pixel_a, pixel_b=pixel_b)
        rest = list(refs[n_in + n_out :])
        w = SimpleNamespace(**{key: rest.pop(0) for key in scratch})
        for v, group in zip(views, buffers[1:]):
            for key in group:
                setattr(v, key, rest.pop(0))
        kernel(views, ins, outs, w)

    vmem = pl.BlockSpec(memory_space=pltpu.VMEM)
    middle = pl.pallas_call(
        body,
        name="step",
        out_shape=(
            jax.ShapeDtypeStruct((H + 16, H), f32),
            jax.ShapeDtypeStruct((K + 16, H), f32),
            jax.ShapeDtypeStruct((C + 16, H), f32),
            jax.ShapeDtypeStruct((8 * ta, 128), f32),
            jax.ShapeDtypeStruct((8 * tb, 128), f32),
        ),
        in_specs=[pl.BlockSpec(memory_space=pl.ANY)] * n_in,
        out_specs=(vmem,) * n_out,
        scratch_shapes=shapes,
        compiler_params=pltpu.CompilerParams(collective_id=0, has_side_effects=True),
    )(*args)
    done = pl.pallas_call(
        finish,
        name="finish",
        out_shape=(
            jax.ShapeDtypeStruct((1, R // nx, C), f32),
            jax.ShapeDtypeStruct((1, C, R // ny), f32),
            jax.ShapeDtypeStruct((1, 1, K, H), f32),
            jax.ShapeDtypeStruct((1, 1, H), f32),
            jax.ShapeDtypeStruct((1, 1, H, H), f32),
            jax.ShapeDtypeStruct((1, 1, H), f32),
            jax.ShapeDtypeStruct((1, 1, C, H), f32),
            jax.ShapeDtypeStruct((1, 1, H), f32),
        ),
        in_specs=[vmem] * n_out,
        out_specs=(vmem,) * 8,
    )(*middle)
    pixel_a, pixel_b, g_in, g_bin, g_mid, g_bmid, g_feat, g_density = done
    return jnp.swapaxes(pixel_a, 1, 2), pixel_b, g_in, g_bin, g_mid, g_bmid, jnp.swapaxes(g_feat, 2, 3), g_density


def solution(mesh):
    block = P("gx", "gy", None, None)
    vector = P("gx", "gy", None)
    in_specs = (block, block, vector, vector)
    in_specs += (P("gy", None), P("gx", None), P("gy", None), P("gx", None))
    in_specs += (P("gy", None, None), P("gx", None, None))
    in_specs += (block, vector, block, vector, block, vector)
    out_specs = (P("gy", None, "gx"), P("gx", None, "gy"))
    out_specs += (block, vector, block, vector, block, vector)
    return jax.shard_map(
        functools.partial(on_device, mesh.shape["gx"], mesh.shape["gy"]),
        mesh=mesh,
        in_specs=in_specs,
        out_specs=out_specs,
        check_vma=False,
    )
```

```python
import functools
from types import SimpleNamespace

import jax
import jax.numpy as jnp
from jax import lax
from jax.experimental import pallas as pl
from jax.experimental.pallas import tpu as pltpu
from jax.sharding import PartitionSpec as P

MESH = pl.DeviceIdType.MESH
f32 = jnp.float32
bf16 = jnp.bfloat16

R = 512
S = 4
C = 64
H = 256
K = 64
OPTICAL_DEPTH = 3.0
PIECE = 256


def dot(a, b):
    return lax.dot_general(a, b, (((1,), (0,)), ((), ())), preferred_element_type=f32)


def dot_t(a, b):
    return lax.dot_general(a, b, (((1,), (1,)), ((), ())), preferred_element_type=f32)


def iota(shape, axis):
    return lax.broadcasted_iota(jnp.int32, shape, axis)


def pack_pixels(chunk):
    t = jnp.transpose(chunk).reshape(8, 2, 8, C)
    return jnp.concatenate([t[:, 0].reshape(64, C), t[:, 1].reshape(64, C)], axis=1)


def unpack_pixels(tiles):
    n = tiles.shape[0] // 8
    low = tiles[:, :C].reshape(n, 1, 8, C)
    high = tiles[:, C:].reshape(n, 1, 8, C)
    return jnp.concatenate([low, high], axis=1).reshape(16 * n, C)


AHEAD = (2, 1, 3, 0)
SEEN_FROM_THERE = (0, 2, 1, 3)


def pack(chunk):
    t = jnp.transpose(chunk)
    return jnp.concatenate([t[:64], t[64:]], axis=1)


def unpack(tiles):
    return jnp.transpose(jnp.concatenate([tiles[:, :C], tiles[:, C:]], axis=0))


def softplus(x):
    e = jnp.exp(-jnp.abs(x))
    z = e / (2.0 + e)
    zz = z * z
    tail = 1 / 3 + zz * (1 / 5 + zz * (1 / 7 + zz * (1 / 9 + zz * (1 / 11 + zz * (1 / 13)))))
    return jnp.maximum(x, 0.0) + 2.0 * z * (1.0 + zz * tail)


def one_minus_exp_neg(x):
    small = 1.0 - x * (1 / 8)
    for k in (7, 6, 5, 4, 3, 2):
        small = 1.0 - x * (1 / k) * small
    return jnp.where(x < 0.5, x * small, 1.0 - jnp.exp(-x))


class View:
    def __init__(self, axis, n, at):
        self.axis = axis
        self.n = n
        self.at = at
        self.delta = OPTICAL_DEPTH / (n * S)
        self.tiles = R // 16 // n
        self.rays = 16 * self.tiles
        self.per_row = 8 // self.tiles


def kernel(views, ins, outs, w):
    a, b = views

    for v in views:
        v.i = lax.axis_index(v.axis)
        own_chunk = v.i // v.per_row
        v.chunks = [lax.rem(own_chunk + ahead, 4) for ahead in AHEAD]
        v.mine = lax.rem(v.i, v.per_row)
        v.peers = []
        for c in range(4):
            for u in range(v.per_row if c < 3 else v.per_row - 1):
                owner = u if c < 3 else lax.rem(v.mine + 1 + u, v.per_row)
                v.peers.append((c, owner, v.chunks[c] * v.per_row + owner))

    barrier = pltpu.get_barrier_semaphore()
    for v in views:
        for _, _, peer in v.peers:
            pl.semaphore_signal(barrier, inc=1, device_id={v.axis: peer}, device_id_type=MESH)

    sem = w.in_sem
    started = []

    def fetch(src, dst):
        copy = pltpu.make_async_copy(src, dst, sem.at[len(started)])
        copy.start()
        started.append(copy)
        return copy

    def fetch_view(v):
        row = pl.multiple_of(v.chunks[3] * 128, 128)
        got = [
            fetch(v.count.at[0], w.count.at[v.at]),
            fetch(v.sign, w.sign.at[v.at]),
            fetch(v.slot, w.slot.at[v.at]),
        ]
        for s in range(S):
            part = v.samples.at[0, 0, :, pl.ds(s * R, R)]
            got.append(fetch(part, w.xs.at[v.at, pl.ds(s * K, K)]))
        v.target_in = fetch(v.target.at[0, :, pl.ds(row, 128)], w.target.at[v.at])
        return got

    got_a = fetch_view(a)
    got_w = [
        fetch(ins.w_in.at[0, 0], w.w_in),
        fetch(ins.b_in.at[0], w.b_in),
        fetch(ins.w_mid.at[0, 0], w.w_mid),
        fetch(ins.b_mid.at[0], w.b_mid),
        fetch(ins.w_feat.at[0, 0], w.w_feat),
        fetch(ins.w_density.at[0], w.w_density),
    ]
    got_b = fetch_view(b)

    for copy in got_w:
        copy.wait()
    w.w_in_t[...] = jnp.transpose(w.w_in[...].astype(f32)).astype(bf16)
    w.w_mid_t[...] = jnp.transpose(w.w_mid[...].astype(f32)).astype(bf16)
    heads = jnp.concatenate(
        [
            w.w_feat[...].astype(f32),
            w.w_density[...].astype(f32),
            jnp.zeros((15, H), f32),
        ],
        axis=0,
    )
    w.heads_t[...] = heads.astype(bf16)
    w.heads[...] = jnp.transpose(heads).astype(bf16)
    w.bias_in[...] = jnp.broadcast_to(jnp.transpose(jnp.broadcast_to(w.b_in[...], (8, H)))[:, :1], (H, 128))
    w.bias_mid[...] = jnp.broadcast_to(jnp.transpose(jnp.broadcast_to(w.b_mid[...], (8, H)))[:, :1], (H, 128))
    ones = jnp.where(iota((16, S * R), 0) == 0, 1.0, 0.0).astype(bf16)

    def arrange(v, got):
        at = v.at
        for copy in got:
            copy.wait()
        counts_signs = [w.count[at].astype(f32), w.sign[at].astype(f32), jnp.zeros((14, R), f32)]
        w.xs[at, S * K : S * K + 16] = jnp.concatenate(counts_signs, axis=0).astype(bf16)
        w.x[at, K : K + 16] = ones
        w.h1[at, H : H + 16] = ones
        rows = iota((8, 128), 0)
        pixels = jnp.concatenate([rows + (16 * u + 8 * h) for h in range(2) for u in range(8)], axis=0)
        slot_row = jnp.broadcast_to(w.slot[at], (16, R)).astype(jnp.int16)
        slot_rows = jnp.concatenate([slot_row] * 16, axis=0)
        for pair in range(2):
            wanted = [pixels + 128 * v.chunks[2 * pair + j] for j in range(2)]
            wanted = jnp.concatenate(wanted, axis=0).astype(jnp.int16)
            wanted = jnp.concatenate([wanted] * 4, axis=1)
            chosen = jnp.where(wanted == slot_rows, jnp.ones((), bf16), jnp.zeros((), bf16))
            moved = dot_t(w.xs[at], chosen)
            for j in range(2):
                c = 2 * pair + j
                lanes = slice(128 * j, 128 * j + 128)
                w.count_row[at, c : c + 1] = moved[S * K : S * K + 1, lanes]
                w.plus[at, c : c + 1] = moved[S * K + 1 : S * K + 2, lanes]
                for s in range(S):
                    here = slice(512 * c + 128 * s, 512 * c + 128 * s + 128)
                    w.x[at, 0:K, here] = moved[s * K : s * K + K, lanes].astype(bf16)
        w.sign_rows[at] = jnp.broadcast_to(w.plus[at, 3:4], (8, 128))

    def forward(v):
        at = v.at
        pieces = [slice(PIECE * p, PIECE * p + PIECE) for p in range(S * R // PIECE)]
        for here in pieces:
            one = dot(w.w_in_t[...], w.x[at, 0:K, here])
            one = (one + jnp.concatenate([w.bias_in[...]] * (PIECE // 128), axis=1)).astype(bf16)
            w.h1[at, 0:H, here] = jnp.maximum(one, jnp.zeros((), bf16))
        for here in pieces:
            two = dot(w.w_mid_t[...], w.h1[at, 0:H, here])
            two = (two + jnp.concatenate([w.bias_mid[...]] * (PIECE // 128), axis=1)).astype(bf16)
            w.h2[at, :, here] = jnp.maximum(two, jnp.zeros((), bf16))
        for c in range(4):
            fd = dot(w.heads_t[...], w.h2[at, :, 512 * c : 512 * c + 512])
            w.feature[at, c] = fd[0:C]
            density = jnp.concatenate([fd[C : C + 1, 128 * s : 128 * s + 128] for s in range(S)], axis=0)
            masked = (iota((S, 128), 0).astype(f32) < w.count_row[at, c : c + 1]).astype(f32)
            optical = v.delta * softplus(density) * masked
            rows = [optical[s : s + 1] for s in range(S)]
            upto = [rows[0]]
            for s in range(1, S):
                upto.append(upto[-1] + rows[s])
            total = upto[-1]
            plus = w.plus[at, c : c + 1] > 0.5
            before = [jnp.where(plus, upto[s] - rows[s], total - upto[s]) for s in range(S)]
            before = jnp.concatenate(before, axis=0)
            weight = jnp.exp(-before) * one_minus_exp_neg(optical)
            w.weight[at, c] = weight
            w.behind_slot[at, c] = jnp.exp(-(before + optical))
            w.slope[at, c] = v.delta * masked * lax.logistic(density)
            w.send_log[at, c] = -total
            colour = weight[0:1] * fd[0:C, 0:128]
            for s in range(1, S):
                colour = colour + weight[s : s + 1] * fd[0:C, 128 * s : 128 * s + 128]
            w.send_colour[at, 64 * c : 64 * c + 64] = pack(colour)

    def start(v, src, dst, k, peer, there=0):
        pltpu.make_async_remote_copy(
            src_ref=src,
            dst_ref=dst.at[v.i],
            send_sem=v.send_sems.at[k],
            recv_sem=v.sems.at[k, there],
            device_id={v.axis: peer},
            device_id_type=MESH,
        ).start()

    def wait(sem, dst, count):
        every = dst.at[pl.ds(0, count)]
        pltpu.make_async_copy(every, every, sem).wait()

    def send_segments(v):
        rows = 8 * v.tiles
        for c, owner, peer in v.peers:
            start(v, w.send_log.at[v.at, c], v.logs, 0, peer)
            first = c * 64 + owner * rows if c < 3 else pl.multiple_of(c * 64 + owner * rows, 8)
            start(v, w.send_colour.at[v.at, pl.ds(first, rows)], v.colours, 1, peer)

    def send_back(v):
        for c, _, peer in v.peers:
            start(v, v.send_aux.at[peer], v.aux, 2, peer, SEEN_FROM_THERE[c])
            start(v, v.send_residual, v.residuals, 3, peer, SEEN_FROM_THERE[c])

    def scan(x, n, back):
        step = 1
        while step < n:
            x = x + pltpu.roll(x, 128 - step if back else step, 1)
            step *= 2
        return x

    def own(v):
        at, i, n = v.at, v.i, v.n
        rows = 8 * v.tiles
        low_part = pl.multiple_of(v.mine * rows, 8)
        high_part = pl.multiple_of(64 + v.mine * rows, 8)
        v.target_in.wait()
        w.tile[...] = pack_pixels(w.target[at])
        target = w.tile[pl.ds(low_part, rows)]
        v.logs[i] = w.send_log[at, 3]
        v.colours[i] = w.send_colour[at, pl.ds(pl.multiple_of(3 * 64 + v.mine * rows, 8), rows)]
        wait(v.sems.at[0, 0], v.logs, n - 1)
        wait(v.sems.at[1, 0], v.colours, n - 1)
        logs = jnp.concatenate(
            [v.logs[...].reshape(n, 128), w.sign_rows[at], jnp.zeros((120 - n, 128), f32)],
            axis=0,
        )
        w.turn[...] = jnp.transpose(logs)
        mine = jnp.concatenate([w.turn[pl.ds(low_part, rows)], w.turn[pl.ds(high_part, rows)]], axis=0)
        lane = iota((v.rays, 128), 1)
        plus = mine[:, n : n + 1] > 0.5
        mine = jnp.where(lane < n, mine, 0.0)

        def beyond(x, ahead):
            low = pltpu.roll(scan(x, n, False), 1, 1)
            high = pltpu.roll(scan(x, n, True), 127, 1)
            return jnp.where(plus, low, high) if ahead else jnp.where(plus, high, low)

        front = jnp.where(lane < n, jnp.exp(beyond(mine, True)), 0.0)
        half = iota((8, 128), 1) < C
        lane8 = iota((8, 128), 1)
        seen_low, seen_high = [], []
        for t in range(v.tiles):
            low, high = front[8 * t : 8 * t + 8], front[rows + 8 * t : rows + 8 * t + 8]
            pixel = None
            for k in range(n):
                part_k = jnp.where(half, low[:, k : k + 1], high[:, k : k + 1])
                part_k = part_k * v.colours[k, 8 * t : 8 * t + 8]
                pixel = part_k if pixel is None else pixel + part_k
            residual = pixel - target[8 * t : 8 * t + 8]
            v.send_residual[8 * t : 8 * t + 8] = residual
            v.pixel[8 * t : 8 * t + 8] = pixel
            sum_low = jnp.zeros((8, 128), f32)
            sum_high = jnp.zeros((8, 128), f32)
            for k in range(n):
                product = residual * v.colours[k, 8 * t : 8 * t + 8]
                at_low = jnp.sum(jnp.where(half, product, 0.0), axis=1, keepdims=True)
                at_high = jnp.sum(jnp.where(half, 0.0, product), axis=1, keepdims=True)
                sum_low = jnp.where(lane8 == k, at_low, sum_low)
                sum_high = jnp.where(lane8 == k, at_high, sum_high)
            seen_low.append(sum_low)
            seen_high.append(sum_high)
        d_log = jnp.where(lane < n, beyond(front * jnp.concatenate(seen_low + seen_high, axis=0), False), 0.0)
        w.turn[...] = jnp.zeros((128, 128), f32)
        both = front + pltpu.roll(d_log, 64, 1)
        w.turn[pl.ds(low_part, rows)] = both[:rows]
        w.turn[pl.ds(high_part, rows)] = both[rows:]
        turned = jnp.transpose(w.turn[...])
        v.send_aux[...] = (turned[0:n] + pltpu.roll(turned[64 : 64 + n], 32, 1)).reshape(n, 1, 128)
        v.aux[i] = v.send_aux[i]
        v.residuals[i] = v.send_residual[...]

    def backward(v, c):
        at, n = v.at, v.per_row
        count = n if c < 3 else n - 1
        wait(v.sems.at[2, c], v.aux, count)
        wait(v.sems.at[3, c], v.residuals, count)
        first = v.chunks[c] * n
        aux = v.aux[pl.ds(first, n)].reshape(n, 128)
        group = lax.rem(iota((n, 128), 1), 64) // (64 // n)
        place = iota((n, 128), 0)
        front = jnp.sum(jnp.where(group == place, aux, 0.0), axis=0, keepdims=True)
        d_log = jnp.sum(jnp.where(group == lax.rem(place + n // 2, n), aux, 0.0), axis=0, keepdims=True)
        d_log = pltpu.roll(jnp.broadcast_to(d_log, (8, 128)), 96, 1)[0:1]
        d_colour = front * unpack(v.residuals[pl.ds(first, n)].reshape(64, 128))
        weight = w.weight[at, c]
        d_weight, d_feature = [], []
        for s in range(S):
            feature = w.feature[at, c, :, 128 * s : 128 * s + 128]
            d_weight.append(jnp.sum(feature * d_colour, axis=0, keepdims=True))
            d_feature.append((weight[s : s + 1] * d_colour).astype(bf16))
        product = [d_weight[s] * weight[s : s + 1] for s in range(S)]
        upto = [product[0]]
        for s in range(1, S):
            upto.append(upto[-1] + product[s])
        plus = w.plus[at, c : c + 1] > 0.5
        d_density = []
        for s in range(S):
            later = jnp.where(plus, upto[-1] - upto[s], upto[s] - product[s])
            d_optical = w.behind_slot[at, c, s : s + 1] * d_weight[s] - d_log - later
            d_density.append(d_optical * w.slope[at, c, s : s + 1])
        d_density = jnp.concatenate(d_density, axis=1)
        d_density = jnp.where(iota((16, 512), 0) == 0, d_density, 0.0).astype(bf16)
        here = slice(512 * c, 512 * c + 512)
        d_heads = jnp.concatenate([jnp.concatenate(d_feature, axis=1), d_density], axis=0)
        w.d_heads[:, here] = d_heads

    def layers_back(v, first, end):
        at = v.at
        pieces = [slice(p, p + PIECE) for p in range(first, end, PIECE)]
        for here in pieces:
            d_two = dot(w.heads[...], w.d_heads[:, here]).astype(bf16)
            w.d_two[:, here] = jnp.where(w.h2[at, :, here] > 0, d_two, jnp.zeros((), bf16))
        for here in pieces:
            d_one = dot(w.w_mid[...], w.d_two[:, here]).astype(bf16)
            w.d_one[:, here] = jnp.where(w.h1[at, 0:H, here] > 0, d_one, jnp.zeros((), bf16))

    def gradients(v, here):
        return (
            dot_t(w.d_heads[:, here], w.h2[v.at, :, here]),
            dot_t(w.h1[v.at, :, here], w.d_two[:, here]),
            dot_t(w.x[v.at, :, here], w.d_one[:, here]),
        )

    arrange(a, got_a)
    forward(a)
    arrange(b, got_b)
    forward(b)
    pl.semaphore_wait(barrier, a.n + b.n - 2)
    send_segments(a)
    send_segments(b)
    own(b)
    send_back(b)
    own(a)
    send_back(a)
    for c in (3, 1, 2, 0):
        backward(b, c)
    layers_back(b, 0, S * R)
    w.g_heads[...], w.g_mid[...], w.g_in[...] = gradients(b, slice(0, S * R))
    for c in (3, 1, 2):
        backward(a, c)
    layers_back(a, R, S * R)
    heads, mid, first = gradients(a, slice(R, S * R))
    w.g_heads[...] += heads
    w.g_mid[...] += mid
    w.g_in[...] += first
    backward(a, 0)
    layers_back(a, 0, R)
    heads, mid, first = gradients(a, slice(0, R))
    outs.mid[...] = w.g_mid[...] + mid
    outs.first[...] = w.g_in[...] + first
    outs.heads[...] = w.g_heads[...] + heads
    outs.pixel_a[...] = a.pixel[...]
    outs.pixel_b[...] = b.pixel[...]
    for v in views:
        for k, dst in enumerate((v.logs, v.colours, v.aux, v.residuals)):
            wait(v.send_sems.at[k], dst, v.n - 1)


def finish(mid, first, heads, pixel_a, pixel_b, o_pa, o_pb, o_win, o_bin, o_wmid, o_bmid, o_wfeat, o_wden):
    o_wmid[0, 0] = mid[0:H]
    o_bmid[0] = mid[H : H + 1]
    o_win[0, 0] = first[0:K]
    o_bin[0] = first[K : K + 1]
    o_wfeat[0, 0] = heads[0:C]
    o_wden[0] = heads[C : C + 1]
    o_pa[0] = unpack_pixels(pixel_a[...])
    o_pb[0] = jnp.transpose(unpack_pixels(pixel_b[...]))


def on_device(nx, ny, *args):
    ta, tb = R // 16 // nx, R // 16 // ny
    args = args[:14] + (jnp.swapaxes(args[14], 2, 3),) + args[15:]
    vm = pltpu.VMEM
    scratch = dict(
        in_sem=pltpu.SemaphoreType.DMA((32,)),
        count=vm((2, 1, R), jnp.int32),
        sign=vm((2, 1, R), jnp.int32),
        slot=vm((2, 1, R), jnp.int32),
        xs=vm((2, S * K + 16, R), bf16),
        target=vm((2, C, 128), f32),
        w_in=vm((K, H), bf16),
        b_in=vm((1, H), f32),
        w_mid=vm((H, H), bf16),
        b_mid=vm((1, H), f32),
        w_feat=vm((C, H), bf16),
        w_density=vm((1, H), bf16),
        w_in_t=vm((H, K), bf16),
        w_mid_t=vm((H, H), bf16),
        heads_t=vm((C + 16, H), bf16),
        heads=vm((H, C + 16), bf16),
        bias_in=vm((H, 128), f32),
        bias_mid=vm((H, 128), f32),
        plus=vm((2, 4, 128), f32),
        count_row=vm((2, 4, 128), f32),
        sign_rows=vm((2, 8, 128), f32),
        x=vm((2, K + 16, S * R), bf16),
        h1=vm((2, H + 16, S * R), bf16),
        h2=vm((2, H, S * R), bf16),
        feature=vm((2, 4, C, S * 128), f32),
        weight=vm((2, 4, S, 128), f32),
        behind_slot=vm((2, 4, S, 128), f32),
        slope=vm((2, 4, S, 128), f32),
        send_log=vm((2, R // 128, 1, 128), f32),
        send_colour=vm((2, R // 2, 128), f32),
        tile=vm((64, 128), f32),
        turn=vm((128, 128), f32),
        d_heads=vm((C + 16, S * R), bf16),
        d_two=vm((H, S * R), bf16),
        d_one=vm((H, S * R), bf16),
        g_mid=vm((H + 16, H), f32),
        g_in=vm((K + 16, H), f32),
        g_heads=vm((C + 16, H), f32),
    )
    def line_buffers(n, tiles):
        return dict(
            pixel=vm((8 * tiles, 128), f32),
            logs=vm((n, 1, 128), f32),
            colours=vm((n, 8 * tiles, 128), f32),
            send_aux=vm((n, 1, 128), f32),
            send_residual=vm((8 * tiles, 128), f32),
            aux=vm((n, 1, 128), f32),
            residuals=vm((n, 8 * tiles, 128), f32),
            sems=pltpu.SemaphoreType.DMA((4, 4)),
            send_sems=pltpu.SemaphoreType.DMA((4,)),
        )

    buffers = (scratch, line_buffers(nx, ta), line_buffers(ny, tb))
    shapes = [shape for group in buffers for shape in group.values()]
    n_in, n_out = len(args), 5

    def body(*refs):
        views = (View("gx", nx, 0), View("gy", ny, 1))
        (
            *by_view,
            w_in,
            b_in,
            w_mid,
            b_mid,
            w_feat,
            w_density,
        ) = refs[:n_in]
        for v in views:
            v.samples, v.count, v.sign, v.slot, v.target = by_view[v.at :: 2]
        ins = SimpleNamespace(w_in=w_in, b_in=b_in, w_mid=w_mid, b_mid=b_mid, w_feat=w_feat, w_density=w_density)
        mid, first, heads, pixel_a, pixel_b = refs[n_in : n_in + n_out]
        outs = SimpleNamespace(mid=mid, first=first, heads=heads, pixel_a=pixel_a, pixel_b=pixel_b)
        rest = list(refs[n_in + n_out :])
        w = SimpleNamespace(**{key: rest.pop(0) for key in scratch})
        for v, group in zip(views, buffers[1:]):
            for key in group:
                setattr(v, key, rest.pop(0))
        kernel(views, ins, outs, w)

    vmem = pl.BlockSpec(memory_space=pltpu.VMEM)
    middle = pl.pallas_call(
        body,
        name="step",
        out_shape=(
            jax.ShapeDtypeStruct((H + 16, H), f32),
            jax.ShapeDtypeStruct((K + 16, H), f32),
            jax.ShapeDtypeStruct((C + 16, H), f32),
            jax.ShapeDtypeStruct((8 * ta, 128), f32),
            jax.ShapeDtypeStruct((8 * tb, 128), f32),
        ),
        in_specs=[pl.BlockSpec(memory_space=pltpu.HBM)] * n_in,
        out_specs=(vmem,) * n_out,
        scratch_shapes=shapes,
        compiler_params=pltpu.CompilerParams(
            collective_id=0, has_side_effects=True
        ),
    )(*args)
    done = pl.pallas_call(
        finish,
        name="finish",
        out_shape=(
            jax.ShapeDtypeStruct((1, R // nx, C), f32),
            jax.ShapeDtypeStruct((1, C, R // ny), f32),
            jax.ShapeDtypeStruct((1, 1, K, H), f32),
            jax.ShapeDtypeStruct((1, 1, H), f32),
            jax.ShapeDtypeStruct((1, 1, H, H), f32),
            jax.ShapeDtypeStruct((1, 1, H), f32),
            jax.ShapeDtypeStruct((1, 1, C, H), f32),
            jax.ShapeDtypeStruct((1, 1, H), f32),
        ),
        in_specs=[vmem] * n_out,
        out_specs=(vmem,) * 8,

    )(*middle)
    pixel_a, pixel_b, g_in, g_bin, g_mid, g_bmid, g_feat, g_density = done
    return jnp.swapaxes(pixel_a, 1, 2), pixel_b, g_in, g_bin, g_mid, g_bmid, jnp.swapaxes(g_feat, 2, 3), g_density


def solution(mesh):
    block = P("gx", "gy", None, None)
    vector = P("gx", "gy", None)
    in_specs = (block, block, vector, vector)
    in_specs += (P("gy", None), P("gx", None), P("gy", None), P("gx", None))
    in_specs += (P("gy", None, None), P("gx", None, None))
    in_specs += (block, vector, block, vector, block, vector)
    out_specs = (P("gy", None, "gx"), P("gx", None, "gy"))
    out_specs += (block, vector, block, vector, block, vector)
    return jax.shard_map(
        functools.partial(on_device, mesh.shape["gx"], mesh.shape["gy"]),
        mesh=mesh,
        in_specs=in_specs,
        out_specs=out_specs,
        check_vma=False,
    )
```

```python
import functools
from types import SimpleNamespace

import jax
import jax.numpy as jnp
from jax import lax
from jax.experimental import pallas as pl
from jax.experimental.pallas import tpu as pltpu
from jax.sharding import PartitionSpec as P

MESH = pl.DeviceIdType.MESH
f32 = jnp.float32
bf16 = jnp.bfloat16

R = 512
S = 4
C = 64
H = 256
K = 64
OPTICAL_DEPTH = 3.0
PIECE = 256


def dot(a, b):
    return lax.dot_general(a, b, (((1,), (0,)), ((), ())), preferred_element_type=f32)


def dot_t(a, b):
    return lax.dot_general(a, b, (((1,), (1,)), ((), ())), preferred_element_type=f32)


def iota(shape, axis):
    return lax.broadcasted_iota(jnp.int32, shape, axis)


def pack_pixels(chunk):
    t = jnp.transpose(chunk).reshape(8, 2, 8, C)
    return jnp.concatenate([t[:, 0].reshape(64, C), t[:, 1].reshape(64, C)], axis=1)


def unpack_pixels(tiles):
    n = tiles.shape[0] // 8
    low = tiles[:, :C].reshape(n, 1, 8, C)
    high = tiles[:, C:].reshape(n, 1, 8, C)
    return jnp.concatenate([low, high], axis=1).reshape(16 * n, C)


AHEAD = (2, 1, 3, 0)
SEEN_FROM_THERE = (0, 2, 1, 3)


def pack(chunk):
    t = jnp.transpose(chunk)
    return jnp.concatenate([t[:64], t[64:]], axis=1)


def unpack(tiles):
    return jnp.transpose(jnp.concatenate([tiles[:, :C], tiles[:, C:]], axis=0))


def softplus(x):
    e = jnp.exp(-jnp.abs(x))
    z = e / (2.0 + e)
    zz = z * z
    tail = 1 / 3 + zz * (1 / 5 + zz * (1 / 7 + zz * (1 / 9 + zz * (1 / 11 + zz * (1 / 13)))))
    return jnp.maximum(x, 0.0) + 2.0 * z * (1.0 + zz * tail)


def one_minus_exp_neg(x):
    small = 1.0 - x * (1 / 8)
    for k in (7, 6, 5, 4, 3, 2):
        small = 1.0 - x * (1 / k) * small
    return jnp.where(x < 0.5, x * small, 1.0 - jnp.exp(-x))


class View:
    def __init__(self, axis, n, at):
        self.axis = axis
        self.n = n
        self.at = at
        self.delta = OPTICAL_DEPTH / (n * S)
        self.tiles = R // 16 // n
        self.rays = 16 * self.tiles
        self.per_row = 8 // self.tiles


def kernel(views, ins, outs, w):
    a, b = views

    for v in views:
        v.i = lax.axis_index(v.axis)
        own_chunk = v.i // v.per_row
        v.chunks = [lax.rem(own_chunk + ahead, 4) for ahead in AHEAD]
        v.mine = lax.rem(v.i, v.per_row)
        v.peers = []
        for c in range(4):
            for u in range(v.per_row if c < 3 else v.per_row - 1):
                owner = u if c < 3 else lax.rem(v.mine + 1 + u, v.per_row)
                v.peers.append((c, owner, v.chunks[c] * v.per_row + owner))

    barrier = pltpu.get_barrier_semaphore()
    for v in views:
        for _, _, peer in v.peers:
            pl.semaphore_signal(barrier, inc=1, device_id={v.axis: peer}, device_id_type=MESH)

    sem = w.in_sem
    started = []

    def fetch(src, dst):
        copy = pltpu.make_async_copy(src, dst, sem.at[len(started)])
        copy.start()
        started.append(copy)
        return copy

    def fetch_view(v):
        row = pl.multiple_of(v.chunks[3] * 128, 128)
        got = [
            fetch(v.count.at[0], w.count.at[v.at]),
            fetch(v.sign, w.sign.at[v.at]),
            fetch(v.slot, w.slot.at[v.at]),
        ]
        for s in range(S):
            part = v.samples.at[0, 0, :, pl.ds(s * R, R)]
            got.append(fetch(part, w.xs.at[v.at, pl.ds(s * K, K)]))
        v.target_in = fetch(v.target.at[0, :, pl.ds(row, 128)], w.target.at[v.at])
        return got

    got_a = fetch_view(a)
    got_w = [
        fetch(ins.w_in.at[0, 0], w.w_in),
        fetch(ins.b_in.at[0], w.b_in),
        fetch(ins.w_mid.at[0, 0], w.w_mid),
        fetch(ins.b_mid.at[0], w.b_mid),
        fetch(ins.w_feat.at[0, 0], w.w_feat),
        fetch(ins.w_density.at[0], w.w_density),
    ]
    got_b = fetch_view(b)

    for copy in got_w:
        copy.wait()
    w.w_in_t[...] = jnp.transpose(w.w_in[...].astype(f32)).astype(bf16)
    w.w_mid_t[...] = jnp.transpose(w.w_mid[...].astype(f32)).astype(bf16)
    heads = jnp.concatenate(
        [
            w.w_feat[...].astype(f32),
            w.w_density[...].astype(f32),
            jnp.zeros((15, H), f32),
        ],
        axis=0,
    )
    w.heads_t[...] = heads.astype(bf16)
    w.heads[...] = jnp.transpose(heads).astype(bf16)
    w.bias_in[...] = jnp.broadcast_to(jnp.transpose(jnp.broadcast_to(w.b_in[...], (8, H)))[:, :1], (H, 128))
    w.bias_mid[...] = jnp.broadcast_to(jnp.transpose(jnp.broadcast_to(w.b_mid[...], (8, H)))[:, :1], (H, 128))
    ones = jnp.where(iota((16, S * R), 0) == 0, 1.0, 0.0).astype(bf16)

    def arrange(v, got):
        at = v.at
        for copy in got:
            copy.wait()
        counts_signs = [w.count[at].astype(f32), w.sign[at].astype(f32), jnp.zeros((14, R), f32)]
        w.xs[at, S * K : S * K + 16] = jnp.concatenate(counts_signs, axis=0).astype(bf16)
        w.x[at, K : K + 16] = ones
        w.h1[at, H : H + 16] = ones
        rows = iota((8, 128), 0)
        pixels = jnp.concatenate([rows + (16 * u + 8 * h) for h in range(2) for u in range(8)], axis=0)
        slot_row = jnp.broadcast_to(w.slot[at], (16, R)).astype(jnp.int16)
        slot_rows = jnp.concatenate([slot_row] * 16, axis=0)
        for pair in range(2):
            wanted = [pixels + 128 * v.chunks[2 * pair + j] for j in range(2)]
            wanted = jnp.concatenate(wanted, axis=0).astype(jnp.int16)
            wanted = jnp.concatenate([wanted] * 4, axis=1)
            chosen = jnp.where(wanted == slot_rows, jnp.ones((), bf16), jnp.zeros((), bf16))
            moved = dot_t(w.xs[at], chosen)
            for j in range(2):
                c = 2 * pair + j
                lanes = slice(128 * j, 128 * j + 128)
                w.count_row[at, c : c + 1] = moved[S * K : S * K + 1, lanes]
                w.plus[at, c : c + 1] = moved[S * K + 1 : S * K + 2, lanes]
                for s in range(S):
                    here = slice(512 * c + 128 * s, 512 * c + 128 * s + 128)
                    w.x[at, 0:K, here] = moved[s * K : s * K + K, lanes].astype(bf16)
        w.sign_rows[at] = jnp.broadcast_to(w.plus[at, 3:4], (8, 128))

    def forward(v):
        at = v.at
        pieces = [slice(PIECE * p, PIECE * p + PIECE) for p in range(S * R // PIECE)]
        for here in pieces:
            one = dot(w.w_in_t[...], w.x[at, 0:K, here])
            one = (one + jnp.concatenate([w.bias_in[...]] * (PIECE // 128), axis=1)).astype(bf16)
            w.h1[at, 0:H, here] = jnp.maximum(one, jnp.zeros((), bf16))
        for here in pieces:
            two = dot(w.w_mid_t[...], w.h1[at, 0:H, here])
            two = (two + jnp.concatenate([w.bias_mid[...]] * (PIECE // 128), axis=1)).astype(bf16)
            w.h2[at, :, here] = jnp.maximum(two, jnp.zeros((), bf16))
        for c in range(4):
            fd = dot(w.heads_t[...], w.h2[at, :, 512 * c : 512 * c + 512])
            w.feature[at, c] = fd[0:C]
            density = jnp.concatenate([fd[C : C + 1, 128 * s : 128 * s + 128] for s in range(S)], axis=0)
            masked = (iota((S, 128), 0).astype(f32) < w.count_row[at, c : c + 1]).astype(f32)
            optical = v.delta * softplus(density) * masked
            rows = [optical[s : s + 1] for s in range(S)]
            upto = [rows[0]]
            for s in range(1, S):
                upto.append(upto[-1] + rows[s])
            total = upto[-1]
            plus = w.plus[at, c : c + 1] > 0.5
            before = [jnp.where(plus, upto[s] - rows[s], total - upto[s]) for s in range(S)]
            before = jnp.concatenate(before, axis=0)
            weight = jnp.exp(-before) * one_minus_exp_neg(optical)
            w.weight[at, c] = weight
            w.behind_slot[at, c] = jnp.exp(-(before + optical))
            w.slope[at, c] = v.delta * masked * lax.logistic(density)
            w.send_log[at, c] = -total
            colour = weight[0:1] * fd[0:C, 0:128]
            for s in range(1, S):
                colour = colour + weight[s : s + 1] * fd[0:C, 128 * s : 128 * s + 128]
            w.send_colour[at, 64 * c : 64 * c + 64] = pack(colour)

    def start(v, src, dst, k, peer, there=0):
        pltpu.make_async_remote_copy(
            src_ref=src,
            dst_ref=dst.at[v.i],
            send_sem=v.send_sems.at[k],
            recv_sem=v.sems.at[k, there],
            device_id={v.axis: peer},
            device_id_type=MESH,
        ).start()

    def wait(sem, dst, count):
        every = dst.at[pl.ds(0, count)]
        pltpu.make_async_copy(every, every, sem).wait()

    def send_segments(v):
        rows = 8 * v.tiles
        for c, owner, peer in v.peers:
            start(v, w.send_log.at[v.at, c], v.logs, 0, peer)
            first = c * 64 + owner * rows if c < 3 else pl.multiple_of(c * 64 + owner * rows, 8)
            start(v, w.send_colour.at[v.at, pl.ds(first, rows)], v.colours, 1, peer)

    def send_back(v):
        for c, _, peer in v.peers:
            start(v, v.send_aux.at[peer], v.aux, 2, peer, SEEN_FROM_THERE[c])
            start(v, v.send_residual, v.residuals, 3, peer, SEEN_FROM_THERE[c])

    def scan(x, n, back):
        step = 1
        while step < n:
            x = x + pltpu.roll(x, 128 - step if back else step, 1)
            step *= 2
        return x

    def own(v):
        at, i, n = v.at, v.i, v.n
        rows = 8 * v.tiles
        low_part = pl.multiple_of(v.mine * rows, 8)
        high_part = pl.multiple_of(64 + v.mine * rows, 8)
        v.target_in.wait()
        w.tile[...] = pack_pixels(w.target[at])
        target = w.tile[pl.ds(low_part, rows)]
        v.logs[i] = w.send_log[at, 3]
        v.colours[i] = w.send_colour[at, pl.ds(pl.multiple_of(3 * 64 + v.mine * rows, 8), rows)]
        wait(v.sems.at[0, 0], v.logs, n - 1)
        wait(v.sems.at[1, 0], v.colours, n - 1)
        logs = jnp.concatenate(
            [v.logs[...].reshape(n, 128), w.sign_rows[at], jnp.zeros((120 - n, 128), f32)],
            axis=0,
        )
        w.turn[...] = jnp.transpose(logs)
        mine = jnp.concatenate([w.turn[pl.ds(low_part, rows)], w.turn[pl.ds(high_part, rows)]], axis=0)
        lane = iota((v.rays, 128), 1)
        plus = mine[:, n : n + 1] > 0.5
        mine = jnp.where(lane < n, mine, 0.0)

        def beyond(x, ahead):
            low = pltpu.roll(scan(x, n, False), 1, 1)
            high = pltpu.roll(scan(x, n, True), 127, 1)
            return jnp.where(plus, low, high) if ahead else jnp.where(plus, high, low)

        front = jnp.where(lane < n, jnp.exp(beyond(mine, True)), 0.0)
        half = iota((8, 128), 1) < C
        lane8 = iota((8, 128), 1)
        seen_low, seen_high = [], []
        for t in range(v.tiles):
            low, high = front[8 * t : 8 * t + 8], front[rows + 8 * t : rows + 8 * t + 8]
            pixel = None
            for k in range(n):
                part_k = jnp.where(half, low[:, k : k + 1], high[:, k : k + 1])
                part_k = part_k * v.colours[k, 8 * t : 8 * t + 8]
                pixel = part_k if pixel is None else pixel + part_k
            residual = pixel - target[8 * t : 8 * t + 8]
            v.send_residual[8 * t : 8 * t + 8] = residual
            v.pixel[8 * t : 8 * t + 8] = pixel
            sum_low = jnp.zeros((8, 128), f32)
            sum_high = jnp.zeros((8, 128), f32)
            for k in range(n):
                product = residual * v.colours[k, 8 * t : 8 * t + 8]
                at_low = jnp.sum(jnp.where(half, product, 0.0), axis=1, keepdims=True)
                at_high = jnp.sum(jnp.where(half, 0.0, product), axis=1, keepdims=True)
                sum_low = jnp.where(lane8 == k, at_low, sum_low)
                sum_high = jnp.where(lane8 == k, at_high, sum_high)
            seen_low.append(sum_low)
            seen_high.append(sum_high)
        d_log = jnp.where(lane < n, beyond(front * jnp.concatenate(seen_low + seen_high, axis=0), False), 0.0)
        w.turn[...] = jnp.zeros((128, 128), f32)
        both = front + pltpu.roll(d_log, 64, 1)
        w.turn[pl.ds(low_part, rows)] = both[:rows]
        w.turn[pl.ds(high_part, rows)] = both[rows:]
        turned = jnp.transpose(w.turn[...])
        v.send_aux[...] = (turned[0:n] + pltpu.roll(turned[64 : 64 + n], 32, 1)).reshape(n, 1, 128)
        v.aux[i] = v.send_aux[i]
        v.residuals[i] = v.send_residual[...]

    def backward(v, c):
        at, n = v.at, v.per_row
        count = n if c < 3 else n - 1
        wait(v.sems.at[2, c], v.aux, count)
        wait(v.sems.at[3, c], v.residuals, count)
        first = v.chunks[c] * n
        aux = v.aux[pl.ds(first, n)].reshape(n, 128)
        group = lax.rem(iota((n, 128), 1), 64) // (64 // n)
        place = iota((n, 128), 0)
        front = jnp.sum(jnp.where(group == place, aux, 0.0), axis=0, keepdims=True)
        d_log = jnp.sum(jnp.where(group == lax.rem(place + n // 2, n), aux, 0.0), axis=0, keepdims=True)
        d_log = pltpu.roll(jnp.broadcast_to(d_log, (8, 128)), 96, 1)[0:1]
        d_colour = front * unpack(v.residuals[pl.ds(first, n)].reshape(64, 128))
        weight = w.weight[at, c]
        d_weight, d_feature = [], []
        for s in range(S):
            feature = w.feature[at, c, :, 128 * s : 128 * s + 128]
            d_weight.append(jnp.sum(feature * d_colour, axis=0, keepdims=True))
            d_feature.append((weight[s : s + 1] * d_colour).astype(bf16))
        product = [d_weight[s] * weight[s : s + 1] for s in range(S)]
        upto = [product[0]]
        for s in range(1, S):
            upto.append(upto[-1] + product[s])
        plus = w.plus[at, c : c + 1] > 0.5
        d_density = []
        for s in range(S):
            later = jnp.where(plus, upto[-1] - upto[s], upto[s] - product[s])
            d_optical = w.behind_slot[at, c, s : s + 1] * d_weight[s] - d_log - later
            d_density.append(d_optical * w.slope[at, c, s : s + 1])
        d_density = jnp.concatenate(d_density, axis=1)
        d_density = jnp.where(iota((16, 512), 0) == 0, d_density, 0.0).astype(bf16)
        here = slice(512 * c, 512 * c + 512)
        d_heads = jnp.concatenate([jnp.concatenate(d_feature, axis=1), d_density], axis=0)
        w.d_heads[:, here] = d_heads

    def layers_back(v, first, end):
        at = v.at
        pieces = [slice(p, p + PIECE) for p in range(first, end, PIECE)]
        for here in pieces:
            d_two = dot(w.heads[...], w.d_heads[:, here]).astype(bf16)
            w.d_two[:, here] = jnp.where(w.h2[at, :, here] > 0, d_two, jnp.zeros((), bf16))
        for here in pieces:
            d_one = dot(w.w_mid[...], w.d_two[:, here]).astype(bf16)
            w.d_one[:, here] = jnp.where(w.h1[at, 0:H, here] > 0, d_one, jnp.zeros((), bf16))

    def gradients(v, here):
        return (
            dot_t(w.d_heads[:, here], w.h2[v.at, :, here]),
            dot_t(w.h1[v.at, :, here], w.d_two[:, here]),
            dot_t(w.x[v.at, :, here], w.d_one[:, here]),
        )

    arrange(a, got_a)
    forward(a)
    arrange(b, got_b)
    forward(b)
    pl.semaphore_wait(barrier, a.n + b.n - 2)
    send_segments(a)
    send_segments(b)
    def put(src, dst, k):
        copy = pltpu.make_async_copy(src, dst, w.out_sem.at[k])
        copy.start()
        return copy

    own(b)
    send_back(b)
    written = [put(b.pixel, outs.pixel_b, 4)]
    own(a)
    send_back(a)
    written.append(put(a.pixel, outs.pixel_a, 3))
    for c in (3, 1, 2, 0):
        backward(b, c)
    layers_back(b, 0, S * R)
    w.g_heads[...], w.g_mid[...], w.g_in[...] = gradients(b, slice(0, S * R))
    for c in (3, 1, 2):
        backward(a, c)
    layers_back(a, R, S * R)
    heads, mid, first = gradients(a, slice(R, S * R))
    w.g_heads[...] += heads
    w.g_mid[...] += mid
    w.g_in[...] += first
    backward(a, 0)
    layers_back(a, 0, R)
    here = slice(0, R)
    w.g_mid[...] += dot_t(w.h1[a.at, :, here], w.d_two[:, here])
    written.append(put(w.g_mid, outs.mid, 0))
    w.g_heads[...] += dot_t(w.d_heads[:, here], w.h2[a.at, :, here])
    written.append(put(w.g_heads, outs.heads, 2))
    w.g_in[...] += dot_t(w.x[a.at, :, here], w.d_one[:, here])
    written.append(put(w.g_in, outs.first, 1))
    for v in views:
        for k, dst in enumerate((v.logs, v.colours, v.aux, v.residuals)):
            wait(v.send_sems.at[k], dst, v.n - 1)
    for copy in written:
        copy.wait()


def finish(mid, first, heads, pixel_a, pixel_b, o_pa, o_pb, o_win, o_bin, o_wmid, o_bmid, o_wfeat, o_wden):
    o_wmid[0, 0] = mid[0:H]
    o_bmid[0] = mid[H : H + 1]
    o_win[0, 0] = first[0:K]
    o_bin[0] = first[K : K + 1]
    o_wfeat[0, 0] = heads[0:C]
    o_wden[0] = heads[C : C + 1]
    o_pa[0] = unpack_pixels(pixel_a[...])
    o_pb[0] = jnp.transpose(unpack_pixels(pixel_b[...]))


def on_device(nx, ny, *args):
    ta, tb = R // 16 // nx, R // 16 // ny
    args = args[:14] + (jnp.swapaxes(args[14], 2, 3),) + args[15:]
    vm = pltpu.VMEM
    scratch = dict(
        in_sem=pltpu.SemaphoreType.DMA((32,)),
        out_sem=pltpu.SemaphoreType.DMA((5,)),
        count=vm((2, 1, R), jnp.int32),
        sign=vm((2, 1, R), jnp.int32),
        slot=vm((2, 1, R), jnp.int32),
        xs=vm((2, S * K + 16, R), bf16),
        target=vm((2, C, 128), f32),
        w_in=vm((K, H), bf16),
        b_in=vm((1, H), f32),
        w_mid=vm((H, H), bf16),
        b_mid=vm((1, H), f32),
        w_feat=vm((C, H), bf16),
        w_density=vm((1, H), bf16),
        w_in_t=vm((H, K), bf16),
        w_mid_t=vm((H, H), bf16),
        heads_t=vm((C + 16, H), bf16),
        heads=vm((H, C + 16), bf16),
        bias_in=vm((H, 128), f32),
        bias_mid=vm((H, 128), f32),
        plus=vm((2, 4, 128), f32),
        count_row=vm((2, 4, 128), f32),
        sign_rows=vm((2, 8, 128), f32),
        x=vm((2, K + 16, S * R), bf16),
        h1=vm((2, H + 16, S * R), bf16),
        h2=vm((2, H, S * R), bf16),
        feature=vm((2, 4, C, S * 128), f32),
        weight=vm((2, 4, S, 128), f32),
        behind_slot=vm((2, 4, S, 128), f32),
        slope=vm((2, 4, S, 128), f32),
        send_log=vm((2, R // 128, 1, 128), f32),
        send_colour=vm((2, R // 2, 128), f32),
        tile=vm((64, 128), f32),
        turn=vm((128, 128), f32),
        d_heads=vm((C + 16, S * R), bf16),
        d_two=vm((H, S * R), bf16),
        d_one=vm((H, S * R), bf16),
        g_mid=vm((H + 16, H), f32),
        g_in=vm((K + 16, H), f32),
        g_heads=vm((C + 16, H), f32),
    )
    def line_buffers(n, tiles):
        return dict(
            pixel=vm((8 * tiles, 128), f32),
            logs=vm((n, 1, 128), f32),
            colours=vm((n, 8 * tiles, 128), f32),
            send_aux=vm((n, 1, 128), f32),
            send_residual=vm((8 * tiles, 128), f32),
            aux=vm((n, 1, 128), f32),
            residuals=vm((n, 8 * tiles, 128), f32),
            sems=pltpu.SemaphoreType.DMA((4, 4)),
            send_sems=pltpu.SemaphoreType.DMA((4,)),
        )

    buffers = (scratch, line_buffers(nx, ta), line_buffers(ny, tb))
    shapes = [shape for group in buffers for shape in group.values()]
    n_in, n_out = len(args), 5

    def body(*refs):
        views = (View("gx", nx, 0), View("gy", ny, 1))
        (
            *by_view,
            w_in,
            b_in,
            w_mid,
            b_mid,
            w_feat,
            w_density,
        ) = refs[:n_in]
        for v in views:
            v.samples, v.count, v.sign, v.slot, v.target = by_view[v.at :: 2]
        ins = SimpleNamespace(w_in=w_in, b_in=b_in, w_mid=w_mid, b_mid=b_mid, w_feat=w_feat, w_density=w_density)
        mid, first, heads, pixel_a, pixel_b = refs[n_in : n_in + n_out]
        outs = SimpleNamespace(mid=mid, first=first, heads=heads, pixel_a=pixel_a, pixel_b=pixel_b)
        rest = list(refs[n_in + n_out :])
        w = SimpleNamespace(**{key: rest.pop(0) for key in scratch})
        for v, group in zip(views, buffers[1:]):
            for key in group:
                setattr(v, key, rest.pop(0))
        kernel(views, ins, outs, w)

    middle = pl.pallas_call(
        body,
        name="step",
        out_shape=(
            jax.ShapeDtypeStruct((H + 16, H), f32),
            jax.ShapeDtypeStruct((K + 16, H), f32),
            jax.ShapeDtypeStruct((C + 16, H), f32),
            jax.ShapeDtypeStruct((8 * ta, 128), f32),
            jax.ShapeDtypeStruct((8 * tb, 128), f32),
        ),
        in_specs=[pl.BlockSpec(memory_space=pltpu.HBM)] * n_in,
        out_specs=(pl.BlockSpec(memory_space=pl.ANY),) * n_out,
        scratch_shapes=shapes,
        compiler_params=pltpu.CompilerParams(
            collective_id=0, has_side_effects=True
        ),
    )(*args)
    done = pl.pallas_call(
        finish,
        name="finish",
        out_shape=(
            jax.ShapeDtypeStruct((1, R // nx, C), f32),
            jax.ShapeDtypeStruct((1, C, R // ny), f32),
            jax.ShapeDtypeStruct((1, 1, K, H), f32),
            jax.ShapeDtypeStruct((1, 1, H), f32),
            jax.ShapeDtypeStruct((1, 1, H, H), f32),
            jax.ShapeDtypeStruct((1, 1, H), f32),
            jax.ShapeDtypeStruct((1, 1, C, H), f32),
            jax.ShapeDtypeStruct((1, 1, H), f32),
        ),
        in_specs=[pl.BlockSpec(memory_space=pltpu.VMEM)] * n_out,
        out_specs=(pl.BlockSpec(memory_space=pltpu.VMEM),) * 8,
    )(*middle)
    pixel_a, pixel_b, g_in, g_bin, g_mid, g_bmid, g_feat, g_density = done
    return jnp.swapaxes(pixel_a, 1, 2), pixel_b, g_in, g_bin, g_mid, g_bmid, jnp.swapaxes(g_feat, 2, 3), g_density


def solution(mesh):
    block = P("gx", "gy", None, None)
    vector = P("gx", "gy", None)
    in_specs = (block, block, vector, vector)
    in_specs += (P("gy", None), P("gx", None), P("gy", None), P("gx", None))
    in_specs += (P("gy", None, None), P("gx", None, None))
    in_specs += (block, vector, block, vector, block, vector)
    out_specs = (P("gy", None, "gx"), P("gx", None, "gy"))
    out_specs += (block, vector, block, vector, block, vector)
    return jax.shard_map(
        functools.partial(on_device, mesh.shape["gx"], mesh.shape["gy"]),
        mesh=mesh,
        in_specs=in_specs,
        out_specs=out_specs,
        check_vma=False,
    )
```
